1024 devices in a mesh: curve: 256 (over x, z, core), group: 4 (over y).
Axes of the slice: x: 4, y: 4, z: 32, core: 2. Of those that a mesh axis runs over, the one named last changes fastest.
Arguments:
- field: float32 [3, 4096, 128, 128], P(None, 'curve', 'group'), may hold values from -6 to 6
- source: float32 [3, 4096, 128, 128], P(None, 'curve', 'group'), may hold values from -16 to 16
- mass: float32 [4096, 128, 128], P('curve', 'group'), may hold values from 0.5 to 8
- interp: float32 [4, 128, 128], replicated, may hold values from -0.5 to 1.5
- parent_list: int32 [256, 4, 4, 16], P('curve', 'group'), may hold values from 0 to 511
- child_list: int32 [256, 4, 4, 16], P('curve', 'group'), may hold values from 0 to 511
- child_kind: int32 [256, 4, 4, 16], P('curve', 'group'), may hold values from 0 to 3
- counts: int32 [256, 4, 4], P('curve', 'group'), may hold values from 0 to 16, as said below
Outputs:
- cycle: float32 [3, 4096, 128, 128], P(None, 'curve', 'group')
The draws below stay inside these ranges and needn't reach their ends.
Inputs may be any that keep to these rules, and one draw needn't show every extreme that they name: `parent_list`: local block index x * 32 + y on the device that owns the parent. `child_list`: local block index x * 32 + y on the device that owns the child. `counts`: in every draw, in each curve segment one destination group receives 16 live slots from every source group; every other destination group receives at most 8 live slots from each source group.
All inputs are finite; a program needn't handle non-finite values.
Results may differ from the reference program's by a relative error of at most 0.0001.
Values sent between devices are 32-bit elements; how exact they have to be, the bound alone decides.
No kernel may reach another device: no remote copies, remote signals or barrier semaphores. Data moves between devices by JAX's collectives and lax.ppermute only.
A program may use at most 32 MiB of HBM per device.

```python
import math
import jax
import jax.numpy as jnp
from jax import lax

NODES = 128
KINDS = 4
SWEEPS = 2
XBLOCKS = 16
YBLOCKS = 32
SLOTS = 16
SEGMENTS = 256
GROUPS = 4
NX = 4096
NY = 128


def draw_interp(key, part):
    noise_key = jax.random.fold_in(key, 11)
    noise = jax.random.uniform(noise_key, (KINDS, NODES, NODES), jnp.float32, -1.0, 1.0)
    identity = jnp.eye(NODES, dtype=jnp.float32)[None]
    return identity + noise * (0.9 / NODES ** 0.5)


def draw_counts(key, part):
    base = jax.random.randint(jax.random.fold_in(key, 21), (SEGMENTS, GROUPS, GROUPS), 0, SLOTS // 2 + 1)
    target = jax.random.randint(jax.random.fold_in(key, 22), (SEGMENTS,), 0, GROUPS)
    filled = jnp.arange(GROUPS)[None, None, :] == target[:, None, None]
    return jnp.where(filled, SLOTS, base).astype(jnp.int32)


def place_ends(array, own_key, low, largest):
    longest = array.shape.index(max(array.shape))
    spots = []
    for shift in (0, 1):
        where = [jax.random.randint(jax.random.fold_in(own_key, axis), (), 0, length) for axis, length in enumerate(array.shape)]
        where[longest] = (where[longest] + shift) % array.shape[longest]
        spots.append(tuple(where))
    return array.at[spots[0]].set(low).at[spots[1]].set(largest)


def level_of(key, extent, cuts, low, high):
    factor_of = 1.0
    for axis_at, parts in cuts:
        draws = jax.random.uniform(jax.random.fold_in(jax.random.fold_in(key, 6), axis_at), (parts,), jnp.float32, low / len(cuts), high / len(cuts))
        factor_of = factor_of * jnp.repeat(jnp.exp(draws), extent[axis_at] // parts).reshape((-1,) + (1,) * (len(extent) - 1 - axis_at))
    return factor_of


def bell_draw(key, extent, width, bound, split=(), kind=jnp.bfloat16):
    values = width * jax.random.normal(key, extent, jnp.float32)
    if split:
        values = values * level_of(key, extent, split, -0.22, 0.18)
    return jnp.clip(values, -bound, bound).astype(kind)


def setup_inputs(seed: int = 0) -> dict:
    splits = jax.random.split(jax.random.key(seed), 9)
    field = bell_draw(splits[0], (3, NX, NY, NODES), 1.0, 6.0, ((1, 256), (2, 4)), jnp.float32)
    source = bell_draw(splits[1], (3, NX, NY, NODES), 4.0, 16.0, ((1, 256), (2, 4)), jnp.float32)
    mass = jnp.clip(jnp.exp(math.log(8.0) - 2.7725887 * jax.random.uniform(splits[2], (NX, NY, NODES), jnp.float32) ** level_of(splits[2], (NX, NY, NODES), ((0, 256), (1, 4)), -0.2, 0.2)), 0.5, 8.0)
    interp = draw_interp(jax.random.fold_in(splits[8], 71), 0)
    parent_list = place_ends(jax.random.randint(splits[4], (SEGMENTS, GROUPS, GROUPS, SLOTS), 0, XBLOCKS * YBLOCKS), jax.random.fold_in(splits[4], 1), 0, (XBLOCKS * YBLOCKS) - 1).astype(jnp.int32)
    child_list = place_ends(jax.random.randint(splits[5], (SEGMENTS, GROUPS, GROUPS, SLOTS), 0, XBLOCKS * YBLOCKS), jax.random.fold_in(splits[5], 1), 0, (XBLOCKS * YBLOCKS) - 1).astype(jnp.int32)
    child_kind = place_ends(jax.random.randint(splits[6], (SEGMENTS, GROUPS, GROUPS, SLOTS), 0, KINDS), jax.random.fold_in(splits[6], 1), 0, KINDS - 1).astype(jnp.int32)
    counts = draw_counts(jax.random.fold_in(splits[8], 71), 0)
    return {"field": field, "source": source, "mass": mass, "interp": interp, "parent_list": parent_list, "child_list": child_list, "child_kind": child_kind, "counts": counts}


OMEGA = 2.0 / 3.0


def relax(padded, source, mass):
    centre = padded[:, 1:-1, 1:-1, :]
    beside = padded[:, 2:, 1:-1, :] + padded[:, :-2, 1:-1, :] + padded[:, 1:-1, 2:, :] + padded[:, 1:-1, :-2, :]
    z_pair = jnp.pad(centre, ((0, 0), (0, 0), (0, 0), (1, 1)))
    beside = beside + z_pair[..., 2:] + z_pair[..., :-2]
    diag_total = 6.0 + mass
    applied = diag_total * centre - beside
    return centre + OMEGA * (source - applied) / diag_total


def to_rows(whole):
    return whole.reshape(3, SEGMENTS, XBLOCKS, GROUPS, YBLOCKS, NODES).transpose(1, 3, 2, 4, 0, 5).reshape(SEGMENTS * GROUPS * XBLOCKS * YBLOCKS, 3, NODES)


def to_field(rows):
    return rows.reshape(SEGMENTS, GROUPS, XBLOCKS, YBLOCKS, 3, NODES).transpose(4, 0, 2, 1, 3, 5).reshape(3, NX, NY, NODES)


def by_kind(picked, tables, kind_faces):
    result = jnp.zeros(picked.shape, jnp.float32)
    flat = picked.reshape(-1, NODES)
    for kind_index in range(KINDS):
        product = jnp.dot(flat, tables[kind_index], precision=lax.Precision.HIGHEST, preferred_element_type=jnp.float32).reshape(picked.shape)
        weight = (kind_faces == kind_index).astype(jnp.float32)
        result = result + product * weight[..., None, None]
    return result


def reference(field, source, mass, interp, parent_list, child_list, child_kind, counts):
    block_count = XBLOCKS * YBLOCKS
    seg_ids = jnp.arange(SEGMENTS, dtype=jnp.int32)[:, None, None, None]
    src_ids = jnp.arange(GROUPS, dtype=jnp.int32)[None, :, None, None]
    dst_ids = jnp.arange(GROUPS, dtype=jnp.int32)[None, None, :, None]
    parent_rows = ((seg_ids * GROUPS + src_ids) * block_count + parent_list).astype(jnp.int32)
    child_faces = jnp.transpose(child_list, (0, 2, 1, 3))
    kind_faces = jnp.transpose(child_kind, (0, 2, 1, 3))
    child_rows = ((seg_ids * GROUPS + dst_ids) * block_count + child_faces).astype(jnp.int32)
    active = (jnp.arange(SLOTS, dtype=jnp.int32)[None, None, None, :] < counts[..., None]).astype(jnp.float32)
    rows = to_rows(field)
    picked = rows[parent_rows] * active[..., None, None]
    hanging = by_kind(picked, interp, kind_faces)
    constrained = to_field(rows.at[child_rows].add(hanging))
    state = constrained
    for sweep_index in range(SWEEPS):
        padded = jnp.pad(state, ((0, 0), (1, 1), (1, 1), (0, 0)))
        state = relax(padded, source, mass)
    correction = to_rows(state - constrained)
    restricted = by_kind(correction[child_rows], jnp.transpose(interp, (0, 2, 1)), kind_faces) * active[..., None, None]
    returned = jnp.zeros_like(rows).at[parent_rows].add(restricted)
    return state + to_field(returned)
```

```python
import jax
import jax.numpy as jnp
from jax import lax
from jax.experimental import pallas as pl
from jax.experimental.pallas import tpu as pltpu
from jax.sharding import PartitionSpec as P

F32 = jnp.float32
BF16 = jnp.bfloat16
OMEGA = 2.0 / 3.0
THIRD = 1.0 / 3.0

PICK = 40
A_EDGE = 3 * PICK
A_PART = A_EDGE + 48
A_DIAG = A_PART + 48
A_CODE = A_DIAG + 16
A_ROWS = A_CODE + 8
B_PART = 96
B_DIAG = 192
B_CORN = 224
B_ROWS = 232

VMEM = pl.BlockSpec(memory_space=pltpu.VMEM)
SMEM = pl.BlockSpec(memory_space=pltpu.SMEM)


def z_pair(a):
    lane = lax.broadcasted_iota(jnp.int32, a.shape, a.ndim - 1)
    low = jnp.where(lane == 0, 0.0, pltpu.roll(a, 1, a.ndim - 1))
    high = jnp.where(lane == 127, 0.0, pltpu.roll(a, 127, a.ndim - 1))
    return low + high


def row_pair(a, before, after):
    n = a.shape[0]
    row = lax.broadcasted_iota(jnp.int32, a.shape, 0)
    low = jnp.where(row == 0, before, pltpu.roll(a, 1, 0))
    high = jnp.where(row == n - 1, after, pltpu.roll(a, n - 1, 0))
    return low + high


def split(a):
    high = a.astype(BF16)
    return high, (a - high.astype(F32)).astype(BF16)


def dot(a, b):
    return jnp.dot(a, b, preferred_element_type=F32)


def dot_t(a, b):
    return lax.dot_general(a, b, (((1,), (1,)), ((), ())), preferred_element_type=F32)


def filled_group(counts):
    target = jnp.int32(0)
    for d in range(1, 4):
        target = jnp.where(counts[0, 0, d] == 16, d, target)
    return target


def column(ref, c, y):
    return ref[c, pl.ds(y, 16, stride=32), :]


def pack(field, source, mass, parents, counts, children, kinds, out, rows):
    g = lax.axis_index("group")
    target = filled_group(counts)
    for d in range(5):
        for k in range(8):
            p = parents[0, 0, d, k] if d < 4 else parents[0, 0, target, 8 + k]
            for c in range(3):
                j = c * PICK + d * 8 + k
                rows[j : j + 1, :] = field[c, pl.ds(p, 1), :]
    slot = lax.broadcasted_iota(jnp.int32, (8, 128), 0)
    for d in range(5):
        live = slot < counts[0, 0, d] if d < 4 else slot + 8 < counts[0, 0, target]
        for c in range(3):
            at = c * PICK + d * 8
            part = jnp.where(live, rows[at : at + 8, :], 0.0)
            for p in range(4):
                out[p, at : at + 8, :] = part
    block = children[0, 0]
    y = block & 31
    x = block >> 5
    sides = []
    for edge, inner, depth in ((0, 1, y), (31, 30, 31 - y)):
        diag = OMEGA / (6.0 + mass[pl.ds(edge, 16, stride=32), :])
        firsts, parts = [], []
        for c in range(3):
            first = column(field, c, edge)
            beside = column(field, c, inner) + row_pair(first, 0.0, 0.0) + z_pair(first)
            firsts.append(first)
            parts.append(first * THIRD + diag * (column(source, c, edge) + beside))
        code = jnp.where(depth < 2, kinds[0, 0] * 32 + depth * 16 + x, -1)
        sides.append((firsts, parts, diag, code.astype(F32)))
    for p in range(4):
        right = p == g + 1
        for c in range(3):
            at = A_EDGE + 16 * c
            out[p, at : at + 16, :] = jnp.where(right, sides[1][0][c], sides[0][0][c])
            at = A_PART + 16 * c
            out[p, at : at + 16, :] = jnp.where(right, sides[1][1][c], sides[0][1][c])
        out[p, A_DIAG : A_DIAG + 16, :] = jnp.where(right, sides[1][2], sides[0][2])
        out[p, A_CODE : A_CODE + 8, :] = jnp.zeros((8, 128), F32)
        out[p, A_CODE : A_CODE + 4, 0:16] = jnp.where(right, sides[1][3], sides[0][3])


def lane_codes(rows):
    total = rows[0:1, :]
    for s in range(1, 4):
        total = total + pltpu.roll(rows[s : s + 1, :], 16 * s, 1)
    return total + pltpu.roll(total, 64, 1)


def selection(codes, start, count, stride):
    place = lax.broadcasted_iota(jnp.int32, (count, 128), 0) + start
    half = lax.broadcasted_iota(jnp.int32, (count, 128), 1) >> 6
    picked = []
    for pair in range(2):
        wanted = (place + (half + 2 * pair) * stride).astype(F32)
        picked.append(jnp.where(codes == wanted, 1.0, 0.0).astype(BF16))
    return jnp.concatenate(picked, axis=1)


def constrain(
    got, field, source, mass, interp, children, kinds, counts, cst, pay1, pay2, near, sweep, ndiag, codes
):
    g = lax.axis_index("group")
    odd = lax.axis_index("curve") & 1
    target = filled_group(counts)
    table = jnp.concatenate([interp[k] for k in range(4)], axis=1)
    table_h, table_l = split(table)

    def contributions(d):
        at = pl.multiple_of(d * 8, 8)
        rows = []
        for c in range(3):
            for s in range(4):
                rows.append(got[s, pl.ds(c * PICK + at, 8), :])
                more = got[s, c * PICK + 32 : c * PICK + 40, :]
                rows.append(jnp.where(target == d, more, 0.0))
        high, low = split(jnp.concatenate(rows, axis=0))
        product = dot(high, table_h) + dot(low, table_h) + dot(high, table_l)
        return split(
            jnp.concatenate(
                [
                    jnp.concatenate(
                        [product[64 * c : 64 * c + 64, 128 * k : 128 * k + 128] for c in range(3)], axis=1
                    )
                    for k in range(4)
                ],
                axis=0,
            )
        )

    codes[...] = jnp.zeros((8, 128), F32)
    codes[0:4, 0:16] = (kinds[0, 0] * 512 + children[0, 0]).astype(F32)
    own = lane_codes(codes)
    high, low = contributions(g)
    for q in range(4):
        chosen = selection(own, q * 128, 128, 512)
        added = dot(chosen, high) + dot(chosen, low)
        for c in range(3):
            rows = slice(q * 128, q * 128 + 128)
            cst[c, rows, :] = field[c, rows, :] + added[:, c * 128 : c * 128 + 128]

    for side in range(2):
        other = g - 1 if side == 0 else g + 1
        exists = (other >= 0) & (other < 4)
        s = jnp.clip(other, 0, 3)
        high, low = contributions(s)
        chosen = selection(lane_codes(got.at[s, A_CODE : A_CODE + 8, :]), 0, 32, 32)
        added = dot(chosen, high) + dot(chosen, low)
        diag = jnp.where(exists, got[s, A_DIAG : A_DIAG + 16, :], 0.0)
        ndiag[side] = diag
        for c in range(3):
            first = added[0:16, c * 128 : c * 128 + 128]
            second = added[16:32, c * 128 : c * 128 + 128]
            edge = got[s, A_EDGE + 16 * c : A_EDGE + 16 * c + 16, :] + first
            near[side, c] = jnp.where(exists, edge, 0.0)
            beside = second + row_pair(first, 0.0, 0.0) + z_pair(first)
            beside = beside + column(cst, c, 0 if side == 0 else 31)
            part = got[s, A_PART + 16 * c : A_PART + 16 * c + 16, :] + first * THIRD
            sweep[side, c] = jnp.where(exists, part + diag * beside, 0.0)

    for pay, upper in ((pay1, 1 - odd), (pay2, odd)):
        edge = upper * 15
        at = pl.multiple_of(edge * 32, 32)
        inner = pl.multiple_of((upper * 13 + 1) * 32, 32)
        diag = OMEGA / (6.0 + mass[pl.ds(at, 32), :])
        pay[B_DIAG : B_DIAG + 32, :] = diag
        pay[B_CORN : B_CORN + 8, :] = jnp.zeros((8, 128), F32)
        for c in range(3):
            first = cst[c, pl.ds(at, 32), :]
            left = near[0, c, pl.ds(edge, 1), :]
            right = near[1, c, pl.ds(edge, 1), :]
            beside = cst[c, pl.ds(inner, 32), :] + row_pair(first, left, right) + z_pair(first)
            pay[32 * c : 32 * c + 32, :] = first
            pay[B_PART + 32 * c : B_PART + 32 * c + 32, :] = first * THIRD + diag * (
                source[c, pl.ds(at, 32), :] + beside
            )
            pay[B_CORN + c : B_CORN + c + 1, :] = left
            pay[B_CORN + 3 + c : B_CORN + 4 + c, :] = right


def smooth(cst, source, mass, near, sweep, children, out, diag, chosen, mid):
    for x in range(16):
        rows = slice(32 * x, 32 * x + 32)
        diag[rows, :] = OMEGA / (6.0 + mass[rows, :])

    def step(state, halo, result):
        for x in range(16):
            rows = slice(32 * x, 32 * x + 32)
            d = diag[rows, :]
            for c in range(3):
                centre = state[c, rows, :]
                beside = row_pair(centre, halo[0, c, x : x + 1, :], halo[1, c, x : x + 1, :]) + z_pair(centre)
                if x > 0:
                    beside = beside + state[c, 32 * x - 32 : 32 * x, :]
                if x < 15:
                    beside = beside + state[c, 32 * x + 32 : 32 * x + 64, :]
                result[c, rows, :] = centre * THIRD + d * (source[c, rows, :] + beside)

    step(cst, near, mid)
    step(mid, sweep, out)
    for s in range(4):
        for k in range(16):
            b = children[0, 0, s, k]
            for c in range(3):
                j = s * 48 + c * 16 + k
                chosen[j : j + 1, :] = out[c, pl.ds(b, 1), :] - cst[c, pl.ds(b, 1), :]


def restrict(chosen, cst, diag, ndiag, got1, got2, interp, children, kinds, fix, out, placed):
    odd = lax.axis_index("curve") & 1
    placed[...] = jnp.zeros(placed.shape, F32)
    for got, upper in ((got1, 1 - odd), (got2, odd)):
        edge = upper * 15
        at = pl.multiple_of(edge * 32, 32)
        inner = pl.multiple_of((upper * 13 + 1) * 32, 32)
        d_edge = diag[pl.ds(at, 32), :]
        d_inner = diag[pl.ds(inner, 32), :]
        far = got[B_DIAG : B_DIAG + 32, :]
        for c in range(3):
            beyond = got[B_PART + 32 * c : B_PART + 32 * c + 32, :] + far * cst[c, pl.ds(at, 32), :]
            first = d_edge * got[32 * c : 32 * c + 32, :]
            left = ndiag[0, pl.ds(edge, 1), :] * got[B_CORN + c : B_CORN + c + 1, :]
            right = ndiag[1, pl.ds(edge, 1), :] * got[B_CORN + 3 + c : B_CORN + 4 + c, :]
            beside = beyond + row_pair(first, left, right) + z_pair(first)
            fix[c, pl.ds(pl.multiple_of(upper * 96, 32), 32), :] = first * THIRD + d_edge * beside
            fix[c, pl.ds(pl.multiple_of(upper * 32 + 32, 32), 32), :] = d_inner * first
    for c in range(3):
        fix[c, 128:136, :] = jnp.zeros((8, 128), F32)
    for s in range(4):
        for k in range(16):
            b = children[0, 0, s, k]
            kind = kinds[0, 0, s, k]
            spot = jnp.where(b < 64, b, jnp.where(b >= 448, b - 384, 128))
            for c in range(3):
                j = s * 48 + c * 16 + k
                placed[kind, pl.ds(j, 1), :] = chosen[j : j + 1, :] + fix[c, pl.ds(spot, 1), :]
    total = None
    for k in range(4):
        high, low = split(placed[k])
        table_h, table_l = split(interp[k])
        product = dot_t(high, table_h) + dot_t(low, table_h) + dot_t(high, table_l)
        total = product if total is None else total + product
    for s in range(4):
        out[s] = total[48 * s : 48 * s + 48, :]


def collect(state, fix, got, parents, counts, out, codes):
    codes[...] = jnp.zeros((8, 128), F32)
    slot = lax.broadcasted_iota(jnp.int32, (1, 16), 1)
    for d in range(4):
        codes[d : d + 1, 0:16] = jnp.where(
            slot < counts[0, 0, d], parents[0, 0, d : d + 1, :], -1
        ).astype(F32)
    total = codes[0:1, :]
    for s in range(1, 4):
        total = total + pltpu.roll(codes[s : s + 1, :], 16 * s, 1)
    rows = jnp.concatenate(
        [
            jnp.concatenate([got[d, 16 * c : 16 * c + 16, :] for d in range(4)], axis=0)
            for c in range(3)
        ],
        axis=1,
    )
    high, low = split(rows)
    place = lax.broadcasted_iota(jnp.int32, (128, 64), 0)
    for q in range(4):
        picked = jnp.where(total[:, 0:64] == (place + q * 128).astype(F32), 1.0, 0.0).astype(BF16)
        added = dot(picked, high) + dot(picked, low)
        for c in range(3):
            at = slice(q * 128, q * 128 + 128)
            result = state[c, at, :] + added[:, c * 128 : c * 128 + 128]
            if q == 0:
                result = jnp.concatenate([result[0:64] + fix[c, 0:64, :], result[64:128]], axis=0)
            if q == 3:
                result = jnp.concatenate([result[0:64], result[64:128] + fix[c, 64:128, :]], axis=0)
            out[c, at, :] = result


def shape(*dims):
    return jax.ShapeDtypeStruct(dims, F32)


def call(body, outs, ins, scratch=(), aliases=None, name=None, flops=1_000_000, moved=1_000_000, limit=16):
    many = isinstance(outs, list)
    return pl.pallas_call(
        body,
        out_shape=outs,
        in_specs=ins,
        out_specs=[VMEM] * len(outs) if many else VMEM,
        scratch_shapes=list(scratch),
        input_output_aliases=aliases or {},
        cost_estimate=pl.CostEstimate(flops=flops, bytes_accessed=moved, transcendentals=0),
        compiler_params=pltpu.CompilerParams(vmem_limit_bytes=limit << 20),
        name=name,
    )


def local(field, source, mass, interp, parents, children, kinds, counts):
    whole = field.shape
    field = field.reshape(3, 512, 128)
    source = source.reshape(3, 512, 128)
    mass = mass.reshape(512, 128)
    send = call(
        pack,
        shape(4, A_ROWS, 128),
        [VMEM, VMEM, VMEM, SMEM, SMEM, VMEM, VMEM],
        [pltpu.VMEM((3 * PICK, 128), F32)],
        name="pack",
    )(field, source, mass, parents, counts, children, kinds)
    got = lax.all_to_all(send, "group", 0, 0, tiled=True)
    cst, pay1, pay2, near, sweep, ndiag = call(
        constrain,
        [
            shape(3, 512, 128),
            shape(B_ROWS, 128),
            shape(B_ROWS, 128),
            shape(2, 3, 16, 128),
            shape(2, 3, 16, 128),
            shape(2, 16, 128),
        ],
        [VMEM] * 7 + [SMEM],
        [pltpu.VMEM((8, 128), F32)],
        name="constrain",
    )(got, field, source, mass, interp, children, kinds, counts)
    count = lax.axis_size("curve")
    inner = [(i, i ^ 1) for i in range(count)]
    outer = [(i, i + 1) for i in range(1, count - 1, 2)]
    outer = outer + [(b, a) for a, b in outer]
    got2 = lax.ppermute(pay2, "curve", outer)
    got1 = lax.ppermute(pay1, "curve", inner)
    state, diag, chosen = call(
        smooth,
        [shape(3, 512, 128), shape(512, 128), shape(192, 128)],
        [VMEM] * 5 + [SMEM],
        [pltpu.VMEM((3, 512, 128), F32)],
        name="smooth",
        flops=20_000_000,
        moved=8_000_000,
    )(cst, source, mass, near, sweep, children)
    fix, send = call(
        restrict,
        [shape(3, 136, 128), shape(4, 48, 128)],
        [VMEM] * 7 + [SMEM, SMEM],
        [pltpu.VMEM((4, 192, 128), F32)],
        name="restrict",
    )(chosen, cst, diag, ndiag, got1, got2, interp, children, kinds)
    got = lax.all_to_all(send, "group", 0, 0, tiled=True)
    out = call(
        collect,
        shape(3, 512, 128),
        [VMEM, VMEM, VMEM, VMEM, SMEM],
        [pltpu.VMEM((8, 128), F32)],
        name="collect",
    )(state, fix, got, parents, counts)
    return out.reshape(whole)


def solution(mesh):
    in_specs = (
        P(None, "curve", "group", None),
        P(None, "curve", "group", None),
        P("curve", "group", None),
        P(),
        P("curve", "group", None, None),
        P("curve", "group", None, None),
        P("curve", "group", None, None),
        P("curve", "group", None),
    )
    out_specs = P(None, "curve", "group", None)
    return jax.shard_map(local, mesh=mesh, in_specs=in_specs, out_specs=out_specs, check_vma=False)
```

```python
import jax
import jax.numpy as jnp
from jax import lax
from jax.experimental import pallas as pl
from jax.experimental.pallas import tpu as pltpu
from jax.sharding import PartitionSpec as P


F32 = jnp.float32
BF16 = jnp.bfloat16
OMEGA = 2.0 / 3.0
THIRD = 1.0 / 3.0

PICK = 32
A_EDGE = 3 * PICK
A_PART = A_EDGE + 48
A_DIAG = A_PART + 48
A_CODE = A_DIAG + 16
A_ROWS = A_CODE + 8
B_PART = 96
B_DIAG = 192
B_CORN = 224
B_ROWS = 232

VMEM = pl.BlockSpec(memory_space=pltpu.VMEM)
SMEM = pl.BlockSpec(memory_space=pltpu.SMEM)
HBM = pl.BlockSpec(memory_space=pltpu.HBM)


def z_pair(a):
    lane = lax.broadcasted_iota(jnp.int32, a.shape, a.ndim - 1)
    low = jnp.where(lane == 0, 0.0, pltpu.roll(a, 1, a.ndim - 1))
    high = jnp.where(lane == 127, 0.0, pltpu.roll(a, 127, a.ndim - 1))
    return low + high


def row_pair(a, before, after):
    n = a.shape[0]
    row = lax.broadcasted_iota(jnp.int32, a.shape, 0)
    low = jnp.where(row == 0, before, pltpu.roll(a, 1, 0))
    high = jnp.where(row == n - 1, after, pltpu.roll(a, n - 1, 0))
    return low + high


def split(a):
    high = a.astype(BF16)
    return high, (a - high.astype(F32)).astype(BF16)


def dot(a, b):
    return jnp.dot(a, b, preferred_element_type=F32)


def dot_t(a, b):
    return lax.dot_general(a, b, (((1,), (1,)), ((), ())), preferred_element_type=F32)


def filled_group(counts):
    target = jnp.int32(0)
    for d in range(1, 4):
        target = jnp.where(counts[0, 0, d] == 16, d, target)
    return target


def column(ref, c, y):
    return ref[c, pl.ds(y, 16, stride=32), :]


def pack(
    field, source, mass, parents, counts, children, kinds, out, codes, f_all,
    s_edge, m_edge, p_scalar, c_scalar, p_lane, child, kind, rows, sems,
):
    copies = [
        pltpu.make_async_copy(parents, p_scalar, sems.at[0]),
        pltpu.make_async_copy(counts, c_scalar, sems.at[1]),
        pltpu.make_async_copy(field.at[0], f_all.at[0], sems.at[2]),
        pltpu.make_async_copy(field.at[1], f_all.at[1], sems.at[3]),
        pltpu.make_async_copy(field.at[2], f_all.at[2], sems.at[4]),
        pltpu.make_async_copy(children, child, sems.at[5]),
        pltpu.make_async_copy(kinds, kind, sems.at[6]),
        pltpu.make_async_copy(parents, p_lane, sems.at[7]),
        pltpu.make_async_copy(source.at[:, :, 0:8, :], s_edge.at[0], sems.at[8]),
        pltpu.make_async_copy(source.at[:, :, 24:32, :], s_edge.at[1], sems.at[9]),
        pltpu.make_async_copy(mass.at[:, 0:8, :], m_edge.at[0], sems.at[10]),
        pltpu.make_async_copy(mass.at[:, 24:32, :], m_edge.at[1], sems.at[11]),
    ]
    for copy in copies:
        copy.start()
    g = lax.axis_index("group")
    for copy in copies[:5]:
        copy.wait()
    target = filled_group(c_scalar)
    for d in range(5):
        for k in range(8):
            p = p_scalar[0, 0, d, k] if d < 4 else p_scalar[0, 0, target, 8 + k]
            for c in range(3):
                j = c * 40 + d * 8 + k
                rows[j : j + 1, :] = f_all[c, pl.ds(p, 1), :]
    slot = lax.broadcasted_iota(jnp.int32, (8, 128), 0)
    for d in range(5):
        live = slot < c_scalar[0, 0, d] if d < 4 else slot + 8 < c_scalar[0, 0, target]
        for c in range(3):
            at = c * 40 + d * 8
            part = jnp.where(live, rows[at : at + 8, :], 0.0)
            for p in range(4):
                near = 3 if d == 4 else d - p + 1
                if 0 <= near < 4 and (d == 4 or near < 3):
                    out[p, c * PICK + near * 8 : c * PICK + near * 8 + 8, :] = part
    for copy in copies[5:]:
        copy.wait()
    block = child[0, 0]
    y = block & 31
    x = block >> 5
    sides = []
    for side, edge, inner, depth in ((0, 0, 1, y), (1, 31, 30, 31 - y)):
        diag = OMEGA / (6.0 + m_edge[side, :, 7 * side, :])
        firsts, parts = [], []
        for c in range(3):
            first = column(f_all, c, edge)
            beside = column(f_all, c, inner) + row_pair(first, 0.0, 0.0) + z_pair(first)
            firsts.append(first)
            parts.append(first * THIRD + diag * (s_edge[side, c, :, 7 * side, :] + beside))
        code = jnp.where(depth < 2, kind[0, 0] * 32 + depth * 16 + x, -1)
        sides.append((firsts, parts, diag, code.astype(F32)))
    for p in range(4):
        right = p == g + 1
        for c in range(3):
            at = A_EDGE + 16 * c
            out[p, at : at + 16, :] = jnp.where(right, sides[1][0][c], sides[0][0][c])
            at = A_PART + 16 * c
            out[p, at : at + 16, :] = jnp.where(right, sides[1][1][c], sides[0][1][c])
        out[p, A_DIAG : A_DIAG + 16, :] = jnp.where(right, sides[1][2], sides[0][2])
        out[p, A_CODE : A_CODE + 8, :] = jnp.zeros((8, 128), F32)
        out[p, A_CODE : A_CODE + 4, 0:16] = jnp.where(right, sides[1][3], sides[0][3])
    codes[...] = jnp.zeros((8, 128), F32)
    slots = lax.broadcasted_iota(jnp.int32, (1, 16), 1)
    for d in range(4):
        codes[d : d + 1, 0:16] = jnp.where(slots < c_scalar[0, 0, d], p_lane[0, 0, d : d + 1, :], -1).astype(F32)


def lane_codes(rows):
    total = rows[0:1, :]
    for s in range(1, 4):
        total = total + pltpu.roll(rows[s : s + 1, :], 16 * s, 1)
    return total + pltpu.roll(total, 64, 1)


def selection(codes, start, count, stride):
    place = lax.broadcasted_iota(jnp.int32, (count, 128), 0) + start
    half = lax.broadcasted_iota(jnp.int32, (count, 128), 1) >> 6
    picked = []
    for pair in range(2):
        wanted = (place + (half + 2 * pair) * stride).astype(F32)
        picked.append(jnp.where(codes == wanted, 1.0, 0.0).astype(BF16))
    return jnp.concatenate(picked, axis=1)


def constrain(
    got, field, source, mass, interp, children, kinds, counts, cst, pay1, pay2, near, sweep, ndiag, codes
):
    g = lax.axis_index("group")
    odd = lax.axis_index("curve") & 1
    target = filled_group(counts)
    table = jnp.concatenate([interp[k] for k in range(4)], axis=1)
    table_h, table_l = split(table)

    def contributions(d, near):
        rows = []
        for c in range(3):
            for s in range(4):
                rows.append(got[s, c * PICK + near * 8 : c * PICK + near * 8 + 8, :])
                more = got[s, c * PICK + 24 : c * PICK + 32, :]
                rows.append(jnp.where(target == d, more, 0.0))
        high, low = split(jnp.concatenate(rows, axis=0))
        product = dot(high, table_h) + dot(low, table_h) + dot(high, table_l)
        return split(
            jnp.concatenate(
                [
                    jnp.concatenate(
                        [product[64 * c : 64 * c + 64, 128 * k : 128 * k + 128] for c in range(3)], axis=1
                    )
                    for k in range(4)
                ],
                axis=0,
            )
        )

    codes[...] = jnp.zeros((8, 128), F32)
    codes[0:4, 0:16] = (kinds[0, 0] * 512 + children[0, 0]).astype(F32)
    own = lane_codes(codes)
    high, low = contributions(g, 1)
    for q in range(4):
        chosen = selection(own, q * 128, 128, 512)
        added = dot(chosen, high) + dot(chosen, low)
        for c in range(3):
            rows = slice(q * 128, q * 128 + 128)
            cst[c, rows, :] = field[c, rows, :] + added[:, c * 128 : c * 128 + 128]

    for side in range(2):
        other = g - 1 if side == 0 else g + 1
        exists = (other >= 0) & (other < 4)
        s = jnp.clip(other, 0, 3)
        high, low = contributions(s, 2 * side)
        chosen = selection(lane_codes(got.at[s, A_CODE : A_CODE + 8, :]), 0, 32, 32)
        added = dot(chosen, high) + dot(chosen, low)
        diag = jnp.where(exists, got[s, A_DIAG : A_DIAG + 16, :], 0.0)
        ndiag[side] = diag
        for c in range(3):
            first = added[0:16, c * 128 : c * 128 + 128]
            second = added[16:32, c * 128 : c * 128 + 128]
            edge = got[s, A_EDGE + 16 * c : A_EDGE + 16 * c + 16, :] + first
            near[side, c] = jnp.where(exists, edge, 0.0)
            beside = second + row_pair(first, 0.0, 0.0) + z_pair(first)
            beside = beside + column(cst, c, 0 if side == 0 else 31)
            part = got[s, A_PART + 16 * c : A_PART + 16 * c + 16, :] + first * THIRD
            sweep[side, c] = jnp.where(exists, part + diag * beside, 0.0)

    for pay, upper in ((pay1, 1 - odd), (pay2, odd)):
        edge = upper * 15
        at = pl.multiple_of(edge * 32, 32)
        inner = pl.multiple_of((upper * 13 + 1) * 32, 32)
        diag = OMEGA / (6.0 + mass[pl.ds(at, 32), :])
        pay[B_DIAG : B_DIAG + 32, :] = diag
        pay[B_CORN : B_CORN + 8, :] = jnp.zeros((8, 128), F32)
        for c in range(3):
            first = cst[c, pl.ds(at, 32), :]
            left = near[0, c, pl.ds(edge, 1), :]
            right = near[1, c, pl.ds(edge, 1), :]
            beside = cst[c, pl.ds(inner, 32), :] + row_pair(first, left, right) + z_pair(first)
            pay[32 * c : 32 * c + 32, :] = first
            pay[B_PART + 32 * c : B_PART + 32 * c + 32, :] = first * THIRD + diag * (
                source[c, pl.ds(at, 32), :] + beside
            )
            pay[B_CORN + c : B_CORN + c + 1, :] = left
            pay[B_CORN + 3 + c : B_CORN + 4 + c, :] = right


def smooth(cst, source, mass, near, sweep, children, out, diag, chosen, mid):
    for x in range(16):
        rows = slice(32 * x, 32 * x + 32)
        diag[rows, :] = OMEGA / (6.0 + mass[rows, :])

    def step(state, halo, result):
        for x in range(16):
            rows = slice(32 * x, 32 * x + 32)
            d = diag[rows, :]
            for c in range(3):
                centre = state[c, rows, :]
                beside = row_pair(centre, halo[0, c, x : x + 1, :], halo[1, c, x : x + 1, :]) + z_pair(centre)
                if x > 0:
                    beside = beside + state[c, 32 * x - 32 : 32 * x, :]
                if x < 15:
                    beside = beside + state[c, 32 * x + 32 : 32 * x + 64, :]
                result[c, rows, :] = centre * THIRD + d * (source[c, rows, :] + beside)

    step(cst, near, mid)
    step(mid, sweep, out)
    for s in range(4):
        for k in range(16):
            b = children[0, 0, s, k]
            for c in range(3):
                j = s * 48 + c * 16 + k
                chosen[j : j + 1, :] = out[c, pl.ds(b, 1), :] - cst[c, pl.ds(b, 1), :]


def restrict(chosen, cst, diag, ndiag, got1, got2, interp, children, kinds, fix, out, placed):
    odd = lax.axis_index("curve") & 1
    placed[...] = jnp.zeros(placed.shape, F32)
    for got, upper in ((got1, 1 - odd), (got2, odd)):
        edge = upper * 15
        at = pl.multiple_of(edge * 32, 32)
        inner = pl.multiple_of((upper * 13 + 1) * 32, 32)
        d_edge = diag[pl.ds(at, 32), :]
        d_inner = diag[pl.ds(inner, 32), :]
        far = got[B_DIAG : B_DIAG + 32, :]
        for c in range(3):
            beyond = got[B_PART + 32 * c : B_PART + 32 * c + 32, :] + far * cst[c, pl.ds(at, 32), :]
            first = d_edge * got[32 * c : 32 * c + 32, :]
            left = ndiag[0, pl.ds(edge, 1), :] * got[B_CORN + c : B_CORN + c + 1, :]
            right = ndiag[1, pl.ds(edge, 1), :] * got[B_CORN + 3 + c : B_CORN + 4 + c, :]
            beside = beyond + row_pair(first, left, right) + z_pair(first)
            fix[c, pl.ds(pl.multiple_of(upper * 96, 32), 32), :] = first * THIRD + d_edge * beside
            fix[c, pl.ds(pl.multiple_of(upper * 32 + 32, 32), 32), :] = d_inner * first
    for c in range(3):
        fix[c, 128:136, :] = jnp.zeros((8, 128), F32)
    for s in range(4):
        for k in range(16):
            b = children[0, 0, s, k]
            kind = kinds[0, 0, s, k]
            spot = jnp.where(b < 64, b, jnp.where(b >= 448, b - 384, 128))
            for c in range(3):
                j = s * 48 + c * 16 + k
                placed[kind, pl.ds(j, 1), :] = chosen[j : j + 1, :] + fix[c, pl.ds(spot, 1), :]
    total = None
    for k in range(4):
        high, low = split(placed[k])
        table_h, table_l = split(interp[k])
        product = dot_t(high, table_h) + dot_t(low, table_h) + dot_t(high, table_l)
        total = product if total is None else total + product
    for s in range(4):
        out[s] = total[48 * s : 48 * s + 48, :]


def collect(state, fix, got, codes, out, result, sems):
    total = codes[0:1, :]
    for s in range(1, 4):
        total = total + pltpu.roll(codes[s : s + 1, :], 16 * s, 1)
    rows = jnp.concatenate(
        [
            jnp.concatenate([got[d, 16 * c : 16 * c + 16, :] for d in range(4)], axis=0)
            for c in range(3)
        ],
        axis=1,
    )
    high, low = split(rows)
    place = lax.broadcasted_iota(jnp.int32, (128, 64), 0)
    copies = []
    for q in range(4):
        picked = jnp.where(total[:, 0:64] == (place + q * 128).astype(F32), 1.0, 0.0).astype(BF16)
        added = dot(picked, high) + dot(picked, low)
        for c in range(3):
            at = slice(q * 128, q * 128 + 128)
            final = state[c, at, :] + added[:, c * 128 : c * 128 + 128]
            if q == 0:
                final = jnp.concatenate([final[0:64] + fix[c, 0:64, :], final[64:128]], axis=0)
            if q == 3:
                final = jnp.concatenate([final[0:64], final[64:128] + fix[c, 64:128, :]], axis=0)
            result[c, at, :] = final
            copy = pltpu.make_async_copy(result.at[c, at, :], out.at[c, at, :], sems.at[len(copies)])
            copy.start()
            copies.append(copy)
    for copy in copies:
        copy.wait()


def stay(array):
    return pltpu.with_memory_space_constraint(array, pltpu.HBM)


def shape(*dims):
    return jax.ShapeDtypeStruct(dims, F32)


def call(body, outs, ins, scratch=(), aliases=None, to=VMEM, flops=1_000_000, moved=1_000_000, limit=16384):
    many = isinstance(outs, list)
    return pl.pallas_call(
        body,
        out_shape=outs,
        in_specs=ins,
        out_specs=[to] * len(outs) if many else to,
        scratch_shapes=list(scratch),
        input_output_aliases=aliases or {},
        cost_estimate=pl.CostEstimate(flops=flops, bytes_accessed=moved, transcendentals=0),
        compiler_params=pltpu.CompilerParams(vmem_limit_bytes=limit << 10),
    )


def local(field, source, mass, interp, parents, children, kinds, counts):
    whole = field.shape
    send, codes, field = call(
        pack,
        [shape(4, A_ROWS, 128), shape(8, 128), shape(3, 512, 128)],
        [HBM] * 7,
        [
            pltpu.VMEM((2, 3, 16, 8, 128), F32),
            pltpu.VMEM((2, 16, 8, 128), F32),
            pltpu.SMEM(parents.shape, jnp.int32),
            pltpu.SMEM(counts.shape, jnp.int32),
            pltpu.VMEM(parents.shape, jnp.int32),
            pltpu.VMEM(parents.shape, jnp.int32),
            pltpu.VMEM(parents.shape, jnp.int32),
            pltpu.VMEM((120, 128), F32),
            pltpu.SemaphoreType.DMA((12,)),
        ],
    )(*map(stay, (field.reshape(3, 512, 128), source, mass, parents, counts, children, kinds)))
    source = source.reshape(3, 512, 128)
    mass = mass.reshape(512, 128)
    got = lax.all_to_all(send, "group", 0, 0, tiled=True)
    cst, pay1, pay2, near, sweep, ndiag = call(
        constrain,
        [
            shape(3, 512, 128),
            shape(B_ROWS, 128),
            shape(B_ROWS, 128),
            shape(2, 3, 16, 128),
            shape(2, 3, 16, 128),
            shape(2, 16, 128),
        ],
        [VMEM] * 7 + [SMEM],
        [pltpu.VMEM((8, 128), F32)],
    )(got, field, source, mass, interp, children, kinds, counts)
    count = lax.axis_size("curve")
    inner = [(i, i ^ 1) for i in range(count)]
    outer = [(i, i + 1) for i in range(1, count - 1, 2)]
    outer = outer + [(b, a) for a, b in outer]
    got2 = lax.ppermute(pay2, "curve", outer)
    got1 = lax.ppermute(pay1, "curve", inner)
    state, diag, chosen = call(
        smooth,
        [shape(3, 512, 128), shape(512, 128), shape(192, 128)],
        [VMEM] * 5 + [SMEM],
        [pltpu.VMEM((3, 512, 128), F32)],
        flops=20_000_000,
        moved=8_000_000,
    )(cst, source, mass, near, sweep, children)
    fix, send = call(
        restrict,
        [shape(3, 136, 128), shape(4, 48, 128)],
        [VMEM] * 7 + [SMEM, SMEM],
        [pltpu.VMEM((4, 192, 128), F32)],
    )(chosen, cst, diag, ndiag, got1, got2, interp, children, kinds)
    got = lax.all_to_all(send, "group", 0, 0, tiled=True)
    out = call(
        collect,
        shape(3, 512, 128),
        [VMEM] * 4,
        [pltpu.VMEM((3, 512, 128), F32), pltpu.SemaphoreType.DMA((12,))],
        to=HBM,
    )(state, fix, got, codes)
    return out.reshape(whole)


def solution(mesh):
    in_specs = (
        P(None, "curve", "group", None),
        P(None, "curve", "group", None),
        P("curve", "group", None),
        P(),
        P("curve", "group", None, None),
        P("curve", "group", None, None),
        P("curve", "group", None, None),
        P("curve", "group", None),
    )
    out_specs = P(None, "curve", "group", None)
    return jax.shard_map(local, mesh=mesh, in_specs=in_specs, out_specs=out_specs, check_vma=False)
```

```python
import functools

import jax
import jax.numpy as jnp
from jax import lax
from jax.experimental import pallas as pl
from jax.experimental.pallas import tpu as pltpu
from jax.sharding import PartitionSpec as P


F32 = jnp.float32
BF16 = jnp.bfloat16
OMEGA = 2.0 / 3.0
THIRD = 1.0 / 3.0

PICK = 32
A_EDGE = 3 * PICK
A_PART = A_EDGE + 48
A_DIAG = A_PART + 48
A_CODE = A_DIAG + 16
A_ROWS = A_CODE + 8
B_PART = 96
B_DIAG = 192
B_CORN = 224
B_ROWS = 232

VMEM = pl.BlockSpec(memory_space=pltpu.VMEM)
SMEM = pl.BlockSpec(memory_space=pltpu.SMEM)
HBM = pl.BlockSpec(memory_space=pltpu.HBM)


def z_pair(a):
    lane = lax.broadcasted_iota(jnp.int32, a.shape, a.ndim - 1)
    low = jnp.where(lane == 0, 0.0, pltpu.roll(a, 1, a.ndim - 1))
    high = jnp.where(lane == 127, 0.0, pltpu.roll(a, 127, a.ndim - 1))
    return low + high


def row_pair(a, before, after):
    n = a.shape[0]
    row = lax.broadcasted_iota(jnp.int32, a.shape, 0)
    low = jnp.where(row == 0, before, pltpu.roll(a, 1, 0))
    high = jnp.where(row == n - 1, after, pltpu.roll(a, n - 1, 0))
    return low + high


def split(a):
    high = a.astype(BF16)
    return high, (a - high.astype(F32)).astype(BF16)


def dot(a, b):
    return jnp.dot(a, b, preferred_element_type=F32)


def dot_t(a, b):
    return lax.dot_general(a, b, (((1,), (1,)), ((), ())), preferred_element_type=F32)


def filled_group(counts):
    target = jnp.int32(0)
    for d in range(1, 4):
        target = jnp.where(counts[0, 0, d] == 16, d, target)
    return target


def column(ref, c, y):
    return ref[c, pl.ds(y, 16, stride=32), :]


def pack(
    field, source, mass, parents, counts, children, kinds, out, codes, f_all,
    s_edge, m_edge, p_scalar, c_scalar, p_lane, child, kind, rows, sems,
):
    copies = [
        pltpu.make_async_copy(parents, p_scalar, sems.at[0]),
        pltpu.make_async_copy(counts, c_scalar, sems.at[1]),
        pltpu.make_async_copy(field.at[0], f_all.at[0], sems.at[2]),
        pltpu.make_async_copy(field.at[1], f_all.at[1], sems.at[3]),
        pltpu.make_async_copy(field.at[2], f_all.at[2], sems.at[4]),
        pltpu.make_async_copy(children, child, sems.at[5]),
        pltpu.make_async_copy(kinds, kind, sems.at[6]),
        pltpu.make_async_copy(parents, p_lane, sems.at[7]),
        pltpu.make_async_copy(source.at[:, :, 0:8, :], s_edge.at[0], sems.at[8]),
        pltpu.make_async_copy(source.at[:, :, 24:32, :], s_edge.at[1], sems.at[9]),
        pltpu.make_async_copy(mass.at[:, 0:8, :], m_edge.at[0], sems.at[10]),
        pltpu.make_async_copy(mass.at[:, 24:32, :], m_edge.at[1], sems.at[11]),
    ]
    for copy in copies:
        copy.start()
    g = lax.axis_index("group")
    for copy in (copies[0], copies[1], *copies[5:8]):
        copy.wait()
    target = filled_group(c_scalar)
    slots = lax.broadcasted_iota(jnp.int32, (1, 16), 1)
    codes[...] = jnp.zeros((24, 128), F32)
    for d in range(4):
        codes[d : d + 1, 0:16] = jnp.where(slots < c_scalar[0, 0, d], p_lane[0, 0, d : d + 1, :], -1).astype(F32)
    codes[8:12, 0:16] = (kind[0, 0] * 512 + child[0, 0]).astype(F32)
    for at in (0, 8):
        codes[at : at + 1, :] = lane_codes(codes.at[at : at + 8, :])
    codes[16:24, :] = jnp.full((8, 128), target.astype(F32))
    for copy in copies[2:5]:
        copy.wait()
    for d in range(5):
        for k in range(8):
            p = p_scalar[0, 0, d, k] if d < 4 else p_scalar[0, 0, target, 8 + k]
            for c in range(3):
                j = c * 40 + d * 8 + k
                rows[j : j + 1, :] = f_all[c, pl.ds(p, 1), :]
    slot = lax.broadcasted_iota(jnp.int32, (8, 128), 0)
    for d in range(5):
        live = slot < c_scalar[0, 0, d] if d < 4 else slot + 8 < c_scalar[0, 0, target]
        for c in range(3):
            at = c * 40 + d * 8
            part = jnp.where(live, rows[at : at + 8, :], 0.0)
            for p in range(4):
                near = 3 if d == 4 else d - p + 1
                if 0 <= near < 4 and (d == 4 or near < 3):
                    out[p, c * PICK + near * 8 : c * PICK + near * 8 + 8, :] = part
    for copy in copies[8:]:
        copy.wait()
    block = child[0, 0]
    y = block & 31
    x = block >> 5
    sides = []
    for side, edge, inner, depth in ((0, 0, 1, y), (1, 31, 30, 31 - y)):
        diag = OMEGA / (6.0 + m_edge[side, :, 7 * side, :])
        firsts, parts = [], []
        for c in range(3):
            first = column(f_all, c, edge)
            beside = column(f_all, c, inner) + row_pair(first, 0.0, 0.0) + z_pair(first)
            firsts.append(first)
            parts.append(first * THIRD + diag * (s_edge[side, c, :, 7 * side, :] + beside))
        code = jnp.where(depth < 2, kind[0, 0] * 32 + depth * 16 + x, -1)
        sides.append((firsts, parts, diag, code.astype(F32)))
    for p in range(4):
        right = p == g + 1
        for c in range(3):
            at = A_EDGE + 16 * c
            out[p, at : at + 16, :] = jnp.where(right, sides[1][0][c], sides[0][0][c])
            at = A_PART + 16 * c
            out[p, at : at + 16, :] = jnp.where(right, sides[1][1][c], sides[0][1][c])
        out[p, A_DIAG : A_DIAG + 16, :] = jnp.where(right, sides[1][2], sides[0][2])
        out[p, A_CODE : A_CODE + 8, :] = jnp.zeros((8, 128), F32)
        out[p, A_CODE : A_CODE + 4, 0:16] = jnp.where(right, sides[1][3], sides[0][3])


def lane_codes(rows):
    total = rows[0:1, :]
    for s in range(1, 4):
        total = total + pltpu.roll(rows[s : s + 1, :], 16 * s, 1)
    return total + pltpu.roll(total, 64, 1)


def selection(codes, start, count, stride):
    place = lax.broadcasted_iota(jnp.int32, (count, 128), 0) + start
    half = lax.broadcasted_iota(jnp.int32, (count, 128), 1) >> 6
    picked = []
    for pair in range(2):
        wanted = (place + (half + 2 * pair) * stride).astype(F32)
        picked.append(jnp.where(codes == wanted, 1.0, 0.0).astype(BF16))
    return jnp.concatenate(picked, axis=1)


def edge_selection(codes):
    place = lax.broadcasted_iota(jnp.int32, (128, 128), 0)
    place = place + jnp.where(place >= 64, 384, 0)
    half = lax.broadcasted_iota(jnp.int32, (128, 128), 1) >> 6
    picked = []
    for pair in range(2):
        wanted = (place + (half + 2 * pair) * 512).astype(F32)
        picked.append(jnp.where(codes == wanted, 1.0, 0.0).T)
    return jnp.concatenate(picked, axis=0).astype(BF16)


def slot_rows(got, near, target, d):
    rows = []
    for c in range(3):
        for s in range(4):
            rows.append(got[s, c * PICK + near * 8 : c * PICK + near * 8 + 8, :])
            more = got[s, c * PICK + 24 : c * PICK + 32, :]
            rows.append(jnp.where(target == d.astype(F32), more, 0.0))
    return jnp.concatenate(rows, axis=0)


def contributions(rows, table_h, table_l):
    high, low = split(rows)
    product = dot(high, table_h) + dot(low, table_h) + dot(high, table_l)
    return split(
        jnp.concatenate(
            [
                jnp.concatenate(
                    [product[64 * c : 64 * c + 64, 128 * k : 128 * k + 128] for c in range(3)], axis=1
                )
                for k in range(4)
            ],
            axis=0,
        )
    )


def stacked(interp):
    return split(jnp.concatenate([interp[k] for k in range(4)], axis=1))


def neighbour(g, side):
    other = g - 1 if side == 0 else g + 1
    return (other >= 0) & (other < 4), jnp.clip(other, 0, 3)


def border(
    got, field, source, mass, interp, codes,
    pay1, pay2, rim, rim_diag, corner_diag, y_high, y_low, corners,
):
    g = lax.axis_index("group")
    odd = lax.axis_index("curve") & 1
    target = codes[16:24, :]
    table_h, table_l = stacked(interp)
    own = codes[8:9, :]
    high, low = contributions(slot_rows(got, 1, target, g), table_h, table_l)
    y_high[...] = high
    y_low[...] = low
    for end, start in ((0, 0), (64, 448)):
        chosen = selection(own, start, 64, 512)
        added = dot(chosen, high) + dot(chosen, low)
        rim_diag[end : end + 64, :] = OMEGA / (6.0 + mass[start : start + 64, :])
        for c in range(3):
            rim[c, end : end + 64, :] = field[c, start : start + 64, :] + added[:, c * 128 : c * 128 + 128]

    corner_diag[...] = jnp.zeros((8, 128), F32)
    line = lax.broadcasted_iota(jnp.int32, (8, 64), 0)
    wanted = ((line >> 1) * 32 + (line & 1) * 15).astype(F32)
    for side in range(2):
        exists, s = neighbour(g, side)
        theirs = lane_codes(got.at[s, A_CODE : A_CODE + 8, :])
        chosen = jnp.where(theirs[:, 0:64] == wanted, 1.0, 0.0).astype(BF16)
        rows = slot_rows(got, 2 * side, target, s)
        high, low = split(jnp.concatenate([rows[64 * c : 64 * c + 64] for c in range(3)], axis=1))
        merged = dot(chosen, high) + dot(chosen, low)
        high, low = split(jnp.concatenate([merged[:, 128 * c : 128 * c + 128] for c in range(3)], axis=0))
        product = dot(high, table_h) + dot(low, table_h) + dot(high, table_l)
        for end in range(2):
            x = 15 * end
            at = 2 * side + end
            corner_diag[at : at + 1, :] = jnp.where(exists, got[s, A_DIAG + x : A_DIAG + x + 1, :], 0.0)
            for c in range(3):
                value = got[s, A_EDGE + 16 * c + x : A_EDGE + 16 * c + x + 1, :]
                for k in range(4):
                    line_at = 8 * c + 2 * k + end
                    value = value + product[line_at : line_at + 1, 128 * k : 128 * k + 128]
                corners[end, 4 * side + c : 4 * side + c + 1, :] = jnp.where(exists, value, 0.0)

    for pay, upper in ((pay1, 1 - odd), (pay2, odd)):
        at = pl.multiple_of(upper * 96, 32)
        inner = pl.multiple_of(upper * 32 + 32, 32)
        whole = pl.multiple_of(upper * 480, 32)
        diag = rim_diag[pl.ds(at, 32), :]
        pay[B_DIAG : B_DIAG + 32, :] = diag
        pay[B_CORN : B_CORN + 8, :] = corners[upper]
        for c in range(3):
            first = rim[c, pl.ds(at, 32), :]
            left = corners[upper, c : c + 1, :]
            right = corners[upper, 4 + c : 5 + c, :]
            beside = rim[c, pl.ds(inner, 32), :] + row_pair(first, left, right) + z_pair(first)
            pay[32 * c : 32 * c + 32, :] = first
            pay[B_PART + 32 * c : B_PART + 32 * c + 32, :] = first * THIRD + diag * (
                source[c, pl.ds(whole, 32), :] + beside
            )


def goes_early():
    c = lax.axis_index("curve")
    return ((c % 64 == 0) & (c > 0)) | (c % 64 == 1)


def smooth(
    early, got, field, source, mass, interp, y_high, y_low, codes, children, kinds, pay,
    state, base, sel, table_h, table_l, passed, cst, mid, near, sweep, diag, child, kind, sems,
):
    passed[...] = pay[...]

    @pl.when(goes_early() == early)
    def _():
        copies = [
            pltpu.make_async_copy(children, child, sems.at[0]),
            pltpu.make_async_copy(kinds, kind, sems.at[1]),
        ]
        for copy in copies:
            copy.start()
        g = lax.axis_index("group")
        target = codes[16:24, :]
        for k in range(4):
            table_h[k], table_l[k] = split(interp[k])
        own = codes[8:9, :]
        sel[...] = edge_selection(own)
        for q in range(4):
            chosen = selection(own, q * 128, 128, 512)
            added = dot(chosen, y_high[...]) + dot(chosen, y_low[...])
            rows = slice(q * 128, q * 128 + 128)
            diag[rows, :] = OMEGA / (6.0 + mass[rows, :])
            for c in range(3):
                cst[c, rows, :] = field[c, rows, :] + added[:, c * 128 : c * 128 + 128]

        stack_h, stack_l = stacked(interp)
        for side in range(2):
            exists, s = neighbour(g, side)
            high, low = contributions(slot_rows(got, 2 * side, target, s), stack_h, stack_l)
            chosen = selection(lane_codes(got.at[s, A_CODE : A_CODE + 8, :]), 0, 32, 32)
            added = dot(chosen, high) + dot(chosen, low)
            beyond = got[s, A_DIAG : A_DIAG + 16, :]
            for c in range(3):
                first = added[0:16, c * 128 : c * 128 + 128]
                second = added[16:32, c * 128 : c * 128 + 128]
                edge = got[s, A_EDGE + 16 * c : A_EDGE + 16 * c + 16, :] + first
                near[side, c] = jnp.where(exists, edge, 0.0)
                beside = second + row_pair(first, 0.0, 0.0) + z_pair(first)
                beside = beside + column(cst, c, 0 if side == 0 else 31)
                part = got[s, A_PART + 16 * c : A_PART + 16 * c + 16, :] + first * THIRD
                sweep[side, c] = jnp.where(exists, part + beyond * beside, 0.0)

        def step(before, halo, result):
            for x in range(16):
                rows = slice(32 * x, 32 * x + 32)
                d = diag[rows, :]
                for c in range(3):
                    centre = before[c, rows, :]
                    beside = row_pair(centre, halo[0, c, x : x + 1, :], halo[1, c, x : x + 1, :]) + z_pair(centre)
                    if x > 0:
                        beside = beside + before[c, 32 * x - 32 : 32 * x, :]
                    if x < 15:
                        beside = beside + before[c, 32 * x + 32 : 32 * x + 64, :]
                    result[c, rows, :] = centre * THIRD + d * (source[c, rows, :] + beside)

        step(cst, near, mid)
        step(mid, sweep, state)
        base[...] = jnp.zeros(base.shape, F32)
        for copy in copies:
            copy.wait()
        for s in range(4):
            for k in range(16):
                b = child[0, 0, s, k]
                row = kind[0, 0, s, k] * 64 + (s * 16 + k)
                for c in range(3):
                    base[c, pl.ds(row, 1), :] = state[c, pl.ds(b, 1), :] - cst[c, pl.ds(b, 1), :]


def restrict(rim, rim_diag, corner_diag, got1, got2, *rest):
    early_set, late_set, (fix, out) = rest[:4], rest[4:8], rest[8:]
    odd = lax.axis_index("curve") & 1
    for got, upper in ((got1, 1 - odd), (got2, odd)):
        at = pl.multiple_of(upper * 96, 32)
        inner = pl.multiple_of(upper * 32 + 32, 32)
        d_edge = rim_diag[pl.ds(at, 32), :]
        d_inner = rim_diag[pl.ds(inner, 32), :]
        far = got[B_DIAG : B_DIAG + 32, :]
        for c in range(3):
            beyond = got[B_PART + 32 * c : B_PART + 32 * c + 32, :] + far * rim[c, pl.ds(at, 32), :]
            first = d_edge * got[32 * c : 32 * c + 32, :]
            left = corner_diag[pl.ds(upper, 1), :] * got[B_CORN + c : B_CORN + c + 1, :]
            right = corner_diag[pl.ds(2 + upper, 1), :] * got[B_CORN + 4 + c : B_CORN + 5 + c, :]
            beside = beyond + row_pair(first, left, right) + z_pair(first)
            fix[c, pl.ds(at, 32), :] = first * THIRD + d_edge * beside
            fix[c, pl.ds(inner, 32), :] = d_inner * first
    high, low = split(jnp.concatenate([fix[c] for c in range(3)], axis=1))

    def finish(base, sel, table_h, table_l):
        rows = dot(sel[...], high) + dot(sel[...], low)
        total = None
        for k in range(4):
            at = slice(64 * k, 64 * k + 64)
            placed = [base[c, at, :] + rows[at, 128 * c : 128 * c + 128] for c in range(3)]
            p_high, p_low = split(jnp.concatenate(placed, axis=0))
            product = dot_t(p_high, table_h[k]) + dot_t(p_low, table_h[k]) + dot_t(p_high, table_l[k])
            total = product if total is None else total + product
        for s in range(4):
            for c in range(3):
                out[s, 16 * c : 16 * c + 16, :] = total[64 * c + 16 * s : 64 * c + 16 * s + 16, :]

    early = goes_early()

    @pl.when(early)
    def _():
        finish(*early_set)

    @pl.when(jnp.logical_not(early))
    def _():
        finish(*late_set)


def collect(early_state, late_state, fix, got, codes, out, result, sems):
    total = codes[0:1, :]
    rows = jnp.concatenate(
        [
            jnp.concatenate([got[d, 16 * c : 16 * c + 16, :] for d in range(4)], axis=0)
            for c in range(3)
        ],
        axis=1,
    )
    high, low = split(rows)
    place = lax.broadcasted_iota(jnp.int32, (128, 64), 0)

    def finish(state):
        copies = []
        for q in range(4):
            picked = jnp.where(total[:, 0:64] == (place + q * 128).astype(F32), 1.0, 0.0).astype(BF16)
            added = dot(picked, high) + dot(picked, low)
            for c in range(3):
                at = slice(q * 128, q * 128 + 128)
                final = state[c, at, :] + added[:, c * 128 : c * 128 + 128]
                if q == 0:
                    final = jnp.concatenate([final[0:64] + fix[c, 0:64, :], final[64:128]], axis=0)
                if q == 3:
                    final = jnp.concatenate([final[0:64], final[64:128] + fix[c, 64:128, :]], axis=0)
                result[c, at, :] = final
                copy = pltpu.make_async_copy(result.at[c, at, :], out.at[c, at, :], sems.at[len(copies)])
                copy.start()
                copies.append(copy)
        for copy in copies:
            copy.wait()

    early = goes_early()

    @pl.when(early)
    def _():
        finish(early_state)

    @pl.when(jnp.logical_not(early))
    def _():
        finish(late_state)


def stay(array):
    return pltpu.with_memory_space_constraint(array, pltpu.HBM)


def shape(*dims, kind=F32):
    return jax.ShapeDtypeStruct(dims, kind)


def call(body, outs, ins, scratch=(), aliases=None, to=VMEM, flops=1_000_000, moved=1_000_000, limit=16384):
    many = isinstance(outs, list)
    return pl.pallas_call(
        body,
        out_shape=outs,
        in_specs=ins,
        out_specs=[to] * len(outs) if many else to,
        scratch_shapes=list(scratch),
        input_output_aliases=aliases or {},
        cost_estimate=pl.CostEstimate(flops=flops, bytes_accessed=moved, transcendentals=0),
        compiler_params=pltpu.CompilerParams(vmem_limit_bytes=limit << 10),
    )


def local(field, source, mass, interp, parents, children, kinds, counts):
    whole = field.shape
    send, codes, field = call(
        pack,
        [shape(4, A_ROWS, 128), shape(24, 128), shape(3, 512, 128)],
        [HBM] * 7,
        [
            pltpu.VMEM((2, 3, 16, 8, 128), F32),
            pltpu.VMEM((2, 16, 8, 128), F32),
            pltpu.SMEM(parents.shape, jnp.int32),
            pltpu.SMEM(counts.shape, jnp.int32),
            pltpu.VMEM(parents.shape, jnp.int32),
            pltpu.VMEM(parents.shape, jnp.int32),
            pltpu.VMEM(parents.shape, jnp.int32),
            pltpu.VMEM((120, 128), F32),
            pltpu.SemaphoreType.DMA((12,)),
        ],
    )(*map(stay, (field.reshape(3, 512, 128), source, mass, parents, counts, children, kinds)))
    source = source.reshape(3, 512, 128)
    mass = mass.reshape(512, 128)
    got = lax.all_to_all(send, "group", 0, 0, tiled=True)
    pay1, pay2, rim, rim_diag, corner_diag, y_high, y_low = call(
        border,
        [
            shape(B_ROWS, 128),
            shape(B_ROWS, 128),
            shape(3, 128, 128),
            shape(128, 128),
            shape(8, 128),
            shape(256, 384, kind=BF16),
            shape(256, 384, kind=BF16),
        ],
        [VMEM] * 6,
        [pltpu.VMEM((2, 8, 128), F32)],
    )(got, field, source, mass, interp, codes)

    def smoothed(early, pay):
        return call(
            functools.partial(smooth, early),
            [
                shape(3, 512, 128),
                shape(3, 256, 128),
                shape(256, 128, kind=BF16),
                shape(4, 128, 128, kind=BF16),
                shape(4, 128, 128, kind=BF16),
                shape(*pay.shape),
            ],
            [VMEM] * 8 + [HBM] * 2 + [VMEM],
            [
                pltpu.VMEM((3, 512, 128), F32),
                pltpu.VMEM((3, 512, 128), F32),
                pltpu.VMEM((2, 3, 16, 128), F32),
                pltpu.VMEM((2, 3, 16, 128), F32),
                pltpu.VMEM((512, 128), F32),
                pltpu.SMEM(children.shape, jnp.int32),
                pltpu.SMEM(kinds.shape, jnp.int32),
                pltpu.SemaphoreType.DMA((2,)),
            ],
            flops=20_000_000,
            moved=8_000_000,
        )(got, field, source, mass, interp, y_high, y_low, codes, stay(children), stay(kinds), pay)

    *early_set, pay2 = smoothed(True, pay2)
    count = lax.axis_size("curve")
    inner = [(i, i ^ 1) for i in range(count)]
    outer = [(i, i + 1) for i in range(1, count - 1, 2)]
    outer = outer + [(b, a) for a, b in outer]
    got2 = lax.ppermute(pay2, "curve", outer)
    got1 = lax.ppermute(pay1, "curve", inner)
    *late_set, _ = smoothed(False, corner_diag)
    fix, send = call(
        restrict, [shape(3, 128, 128), shape(4, 48, 128)], [VMEM] * 13
    )(rim, rim_diag, corner_diag, got1, got2, *early_set[1:], *late_set[1:])
    got = lax.all_to_all(send, "group", 0, 0, tiled=True)
    out = call(
        collect,
        shape(3, 512, 128),
        [VMEM] * 5,
        [pltpu.VMEM((3, 512, 128), F32), pltpu.SemaphoreType.DMA((12,))],
        to=HBM,
    )(early_set[0], late_set[0], fix, got, codes)
    return out.reshape(whole)


def solution(mesh):
    in_specs = (
        P(None, "curve", "group", None),
        P(None, "curve", "group", None),
        P("curve", "group", None),
        P(),
        P("curve", "group", None, None),
        P("curve", "group", None, None),
        P("curve", "group", None, None),
        P("curve", "group", None),
    )
    out_specs = P(None, "curve", "group", None)
    return jax.shard_map(local, mesh=mesh, in_specs=in_specs, out_specs=out_specs, check_vma=False)
```

```python
import functools

import jax
import jax.numpy as jnp
from jax import lax
from jax.experimental import pallas as pl
from jax.experimental.pallas import tpu as pltpu
from jax.sharding import PartitionSpec as P


F32 = jnp.float32
BF16 = jnp.bfloat16
OMEGA = 2.0 / 3.0
THIRD = 1.0 / 3.0

PICK = 32
A_EDGE = 3 * PICK
A_PART = A_EDGE + 48
A_DIAG = A_PART + 48
A_CODE = A_DIAG + 16
A_ROWS = A_CODE + 8
B_PART = 96
B_DIAG = 192
B_CORN = 224
B_ROWS = 232

VMEM = pl.BlockSpec(memory_space=pltpu.VMEM)
SMEM = pl.BlockSpec(memory_space=pltpu.SMEM)
HBM = pl.BlockSpec(memory_space=pltpu.HBM)


def z_pair(a):
    lane = lax.broadcasted_iota(jnp.int32, a.shape, a.ndim - 1)
    low = jnp.where(lane == 0, 0.0, pltpu.roll(a, 1, a.ndim - 1))
    high = jnp.where(lane == 127, 0.0, pltpu.roll(a, 127, a.ndim - 1))
    return low + high


def row_pair(a, before, after):
    n = a.shape[0]
    row = lax.broadcasted_iota(jnp.int32, a.shape, 0)
    low = jnp.where(row == 0, before, pltpu.roll(a, 1, 0))
    high = jnp.where(row == n - 1, after, pltpu.roll(a, n - 1, 0))
    return low + high


def split(a):
    high = a.astype(BF16)
    return high, (a - high.astype(F32)).astype(BF16)


def dot(a, b):
    return jnp.dot(a, b, preferred_element_type=F32)


def dot_t(a, b):
    return lax.dot_general(a, b, (((1,), (1,)), ((), ())), preferred_element_type=F32)


def filled_group(counts):
    target = jnp.int32(0)
    for d in range(1, 4):
        target = jnp.where(counts[0, 0, d] == 16, d, target)
    return target


def column(ref, c, y):
    return ref[c, pl.ds(y, 16, stride=32), :]


def pack(
    field, source, mass, parents, counts, children, kinds, out, codes, f_all, m_all,
    s_edge, p_scalar, c_scalar, p_lane, child, kind, rows, sems,
):
    copies = [
        pltpu.make_async_copy(parents, p_scalar, sems.at[0]),
        pltpu.make_async_copy(counts, c_scalar, sems.at[1]),
        pltpu.make_async_copy(field.at[0], f_all.at[0], sems.at[2]),
        pltpu.make_async_copy(field.at[1], f_all.at[1], sems.at[3]),
        pltpu.make_async_copy(field.at[2], f_all.at[2], sems.at[4]),
        pltpu.make_async_copy(children, child, sems.at[5]),
        pltpu.make_async_copy(kinds, kind, sems.at[6]),
        pltpu.make_async_copy(parents, p_lane, sems.at[7]),
        pltpu.make_async_copy(source.at[:, :, 0, :], s_edge.at[0], sems.at[8]),
        pltpu.make_async_copy(source.at[:, :, 31, :], s_edge.at[1], sems.at[9]),
        pltpu.make_async_copy(mass, m_all, sems.at[10]),
    ]
    for copy in copies:
        copy.start()
    g = lax.axis_index("group")
    for copy in (copies[0], copies[1], *copies[5:8]):
        copy.wait()
    target = filled_group(c_scalar)
    slots = lax.broadcasted_iota(jnp.int32, (1, 16), 1)
    codes[...] = jnp.zeros((24, 128), F32)
    for d in range(4):
        codes[d : d + 1, 0:16] = jnp.where(slots < c_scalar[0, 0, d], p_lane[0, 0, d : d + 1, :], -1).astype(F32)
    codes[8:12, 0:16] = (kind[0, 0] * 512 + child[0, 0]).astype(F32)
    for at in (0, 8):
        codes[at : at + 1, :] = lane_codes(codes.at[at : at + 8, :])
    codes[16:24, :] = jnp.full((8, 128), target.astype(F32))
    for copy in copies[2:5]:
        copy.wait()
    for d in range(5):
        for k in range(8):
            p = p_scalar[0, 0, d, k] if d < 4 else p_scalar[0, 0, target, 8 + k]
            for c in range(3):
                j = c * 40 + d * 8 + k
                rows[j : j + 1, :] = f_all[c, pl.ds(p, 1), :]
    slot = lax.broadcasted_iota(jnp.int32, (8, 128), 0)
    for d in range(5):
        live = slot < c_scalar[0, 0, d] if d < 4 else slot + 8 < c_scalar[0, 0, target]
        for c in range(3):
            at = c * 40 + d * 8
            part = jnp.where(live, rows[at : at + 8, :], 0.0)
            for p in range(4):
                near = 3 if d == 4 else d - p + 1
                if 0 <= near < 4 and (d == 4 or near < 3):
                    out[p, c * PICK + near * 8 : c * PICK + near * 8 + 8, :] = part
    for copy in copies[8:]:
        copy.wait()
    block = child[0, 0]
    y = block & 31
    x = block >> 5
    sides = []
    for side, edge, inner, depth in ((0, 0, 1, y), (1, 31, 30, 31 - y)):
        diag = OMEGA / (6.0 + m_all[pl.ds(edge, 16, stride=32), :])
        firsts, parts = [], []
        for c in range(3):
            first = column(f_all, c, edge)
            beside = column(f_all, c, inner) + row_pair(first, 0.0, 0.0) + z_pair(first)
            firsts.append(first)
            parts.append(first * THIRD + diag * (s_edge[side, c] + beside))
        code = jnp.where(depth < 2, kind[0, 0] * 32 + depth * 16 + x, -1)
        sides.append((firsts, parts, diag, code.astype(F32)))
    for p in range(4):
        right = p == g + 1
        for c in range(3):
            at = A_EDGE + 16 * c
            out[p, at : at + 16, :] = jnp.where(right, sides[1][0][c], sides[0][0][c])
            at = A_PART + 16 * c
            out[p, at : at + 16, :] = jnp.where(right, sides[1][1][c], sides[0][1][c])
        out[p, A_DIAG : A_DIAG + 16, :] = jnp.where(right, sides[1][2], sides[0][2])
        out[p, A_CODE : A_CODE + 8, :] = jnp.zeros((8, 128), F32)
        out[p, A_CODE : A_CODE + 4, 0:16] = jnp.where(right, sides[1][3], sides[0][3])


def lane_codes(rows):
    total = rows[0:1, :]
    for s in range(1, 4):
        total = total + pltpu.roll(rows[s : s + 1, :], 16 * s, 1)
    return total + pltpu.roll(total, 64, 1)


def selection(codes, start, count, stride):
    place = lax.broadcasted_iota(jnp.int32, (count, 128), 0) + start
    half = lax.broadcasted_iota(jnp.int32, (count, 128), 1) >> 6
    picked = []
    for pair in range(2):
        wanted = (place + (half + 2 * pair) * stride).astype(F32)
        picked.append(jnp.where(codes == wanted, 1.0, 0.0).astype(BF16))
    return jnp.concatenate(picked, axis=1)


def edge_selection(codes):
    place = lax.broadcasted_iota(jnp.int32, (128, 128), 0)
    place = place + jnp.where(place >= 64, 384, 0)
    half = lax.broadcasted_iota(jnp.int32, (128, 128), 1) >> 6
    picked = []
    for pair in range(2):
        wanted = (place + (half + 2 * pair) * 512).astype(F32)
        picked.append(jnp.where(codes == wanted, 1.0, 0.0).T)
    return jnp.concatenate(picked, axis=0).astype(BF16)


def slot_rows(got, near, target, d):
    rows = []
    for c in range(3):
        for s in range(4):
            rows.append(got[s, c * PICK + near * 8 : c * PICK + near * 8 + 8, :])
            more = got[s, c * PICK + 24 : c * PICK + 32, :]
            rows.append(jnp.where(target == d.astype(F32), more, 0.0))
    return jnp.concatenate(rows, axis=0)


def contributions(rows, table_h, table_l):
    high, low = split(rows)
    product = dot(high, table_h) + dot(low, table_h) + dot(high, table_l)
    return split(
        jnp.concatenate(
            [
                jnp.concatenate(
                    [product[64 * c : 64 * c + 64, 128 * k : 128 * k + 128] for c in range(3)], axis=1
                )
                for k in range(4)
            ],
            axis=0,
        )
    )


def stacked(interp):
    return split(jnp.concatenate([interp[k] for k in range(4)], axis=1))


def neighbour(g, side):
    other = g - 1 if side == 0 else g + 1
    return (other >= 0) & (other < 4), jnp.clip(other, 0, 3)


def border(
    got, field, source, mass, interp, codes,
    pay1, pay2, rim, rim_diag, corner_diag, y_high, y_low, corners,
):
    g = lax.axis_index("group")
    odd = lax.axis_index("curve") & 1
    target = codes[16:24, :]
    table_h, table_l = stacked(interp)
    own = codes[8:9, :]
    high, low = contributions(slot_rows(got, 1, target, g), table_h, table_l)
    y_high[...] = high
    y_low[...] = low
    for end, start in ((0, 0), (64, 448)):
        chosen = selection(own, start, 64, 512)
        added = dot(chosen, high) + dot(chosen, low)
        rim_diag[end : end + 64, :] = OMEGA / (6.0 + mass[start : start + 64, :])
        for c in range(3):
            rim[c, end : end + 64, :] = field[c, start : start + 64, :] + added[:, c * 128 : c * 128 + 128]

    corner_diag[...] = jnp.zeros((8, 128), F32)
    line = lax.broadcasted_iota(jnp.int32, (8, 64), 0)
    wanted = ((line >> 1) * 32 + (line & 1) * 15).astype(F32)
    for side in range(2):
        exists, s = neighbour(g, side)
        theirs = lane_codes(got.at[s, A_CODE : A_CODE + 8, :])
        chosen = jnp.where(theirs[:, 0:64] == wanted, 1.0, 0.0).astype(BF16)
        rows = slot_rows(got, 2 * side, target, s)
        high, low = split(jnp.concatenate([rows[64 * c : 64 * c + 64] for c in range(3)], axis=1))
        merged = dot(chosen, high) + dot(chosen, low)
        high, low = split(jnp.concatenate([merged[:, 128 * c : 128 * c + 128] for c in range(3)], axis=0))
        product = dot(high, table_h) + dot(low, table_h) + dot(high, table_l)
        for end in range(2):
            x = 15 * end
            at = 2 * side + end
            corner_diag[at : at + 1, :] = jnp.where(exists, got[s, A_DIAG + x : A_DIAG + x + 1, :], 0.0)
            for c in range(3):
                value = got[s, A_EDGE + 16 * c + x : A_EDGE + 16 * c + x + 1, :]
                for k in range(4):
                    line_at = 8 * c + 2 * k + end
                    value = value + product[line_at : line_at + 1, 128 * k : 128 * k + 128]
                corners[end, 4 * side + c : 4 * side + c + 1, :] = jnp.where(exists, value, 0.0)

    for pay, upper in ((pay1, 1 - odd), (pay2, odd)):
        at = pl.multiple_of(upper * 96, 32)
        inner = pl.multiple_of(upper * 32 + 32, 32)
        whole = pl.multiple_of(upper * 480, 32)
        diag = rim_diag[pl.ds(at, 32), :]
        pay[B_DIAG : B_DIAG + 32, :] = diag
        pay[B_CORN : B_CORN + 8, :] = corners[upper]
        for c in range(3):
            first = rim[c, pl.ds(at, 32), :]
            left = corners[upper, c : c + 1, :]
            right = corners[upper, 4 + c : 5 + c, :]
            beside = rim[c, pl.ds(inner, 32), :] + row_pair(first, left, right) + z_pair(first)
            pay[32 * c : 32 * c + 32, :] = first
            pay[B_PART + 32 * c : B_PART + 32 * c + 32, :] = first * THIRD + diag * (
                source[c, pl.ds(whole, 32), :] + beside
            )


def waits():
    c = lax.axis_index("curve")
    return (c >= 64) & (c % 64 < 2)


def goes_early():
    c = lax.axis_index("curve")
    return ((c % 64 == 0) & (c > 0)) | (c % 64 == 1)


def smooth(early, got, field, source, mass, interp, y_high, y_low, codes, children, kinds, *rest):
    if early:
        pay, *rest = rest
        state, base, sel, table_h, table_l, passed, cst, mid, near, sweep, diag, child, kind, sems = rest
        passed[...] = pay[...]
    else:
        state, base, sel, table_h, table_l, cst, mid, near, sweep, diag, child, kind, sems = rest

    @pl.when(goes_early() == early)
    def _():
        copies = [
            pltpu.make_async_copy(children, child, sems.at[0]),
            pltpu.make_async_copy(kinds, kind, sems.at[1]),
        ]
        for copy in copies:
            copy.start()
        g = lax.axis_index("group")
        target = codes[16:24, :]
        for k in range(4):
            table_h[k], table_l[k] = split(interp[k])
        own = codes[8:9, :]
        sel[...] = edge_selection(own)
        for q in range(4):
            chosen = selection(own, q * 128, 128, 512)
            added = dot(chosen, y_high[...]) + dot(chosen, y_low[...])
            rows = slice(q * 128, q * 128 + 128)
            diag[rows, :] = OMEGA / (6.0 + mass[rows, :])
            for c in range(3):
                cst[c, rows, :] = field[c, rows, :] + added[:, c * 128 : c * 128 + 128]

        stack_h, stack_l = stacked(interp)
        for side in range(2):
            exists, s = neighbour(g, side)
            high, low = contributions(slot_rows(got, 2 * side, target, s), stack_h, stack_l)
            chosen = selection(lane_codes(got.at[s, A_CODE : A_CODE + 8, :]), 0, 32, 32)
            added = dot(chosen, high) + dot(chosen, low)
            beyond = got[s, A_DIAG : A_DIAG + 16, :]
            for c in range(3):
                first = added[0:16, c * 128 : c * 128 + 128]
                second = added[16:32, c * 128 : c * 128 + 128]
                edge = got[s, A_EDGE + 16 * c : A_EDGE + 16 * c + 16, :] + first
                near[side, c] = jnp.where(exists, edge, 0.0)
                beside = second + row_pair(first, 0.0, 0.0) + z_pair(first)
                beside = beside + column(cst, c, 0 if side == 0 else 31)
                part = got[s, A_PART + 16 * c : A_PART + 16 * c + 16, :] + first * THIRD
                sweep[side, c] = jnp.where(exists, part + beyond * beside, 0.0)

        def step(before, halo, result):
            for x in range(16):
                rows = slice(32 * x, 32 * x + 32)
                d = diag[rows, :]
                for c in range(3):
                    centre = before[c, rows, :]
                    beside = row_pair(centre, halo[0, c, x : x + 1, :], halo[1, c, x : x + 1, :]) + z_pair(centre)
                    if x > 0:
                        beside = beside + before[c, 32 * x - 32 : 32 * x, :]
                    if x < 15:
                        beside = beside + before[c, 32 * x + 32 : 32 * x + 64, :]
                    result[c, rows, :] = centre * THIRD + d * (source[c, rows, :] + beside)

        step(cst, near, mid)
        step(mid, sweep, state)
        base[...] = jnp.zeros(base.shape, F32)
        for copy in copies:
            copy.wait()
        for s in range(4):
            for k in range(16):
                b = child[0, 0, s, k]
                row = kind[0, 0, s, k] * 64 + (s * 16 + k)
                for c in range(3):
                    base[c, pl.ds(row, 1), :] = state[c, pl.ds(b, 1), :] - cst[c, pl.ds(b, 1), :]


def restrict(rim, rim_diag, corner_diag, got_first, got_last, got2, *rest):
    early_set, late_set, (fix, out) = rest[:4], rest[4:8], rest[8:]
    odd = lax.axis_index("curve") & 1
    got1 = jnp.where(waits(), got_first[...], got_last[...])
    for got, upper in ((got1, 1 - odd), (got2[...], odd)):
        at = pl.multiple_of(upper * 96, 32)
        inner = pl.multiple_of(upper * 32 + 32, 32)
        d_edge = rim_diag[pl.ds(at, 32), :]
        d_inner = rim_diag[pl.ds(inner, 32), :]
        far = got[B_DIAG : B_DIAG + 32, :]
        for c in range(3):
            beyond = got[B_PART + 32 * c : B_PART + 32 * c + 32, :] + far * rim[c, pl.ds(at, 32), :]
            first = d_edge * got[32 * c : 32 * c + 32, :]
            left = corner_diag[pl.ds(upper, 1), :] * got[B_CORN + c : B_CORN + c + 1, :]
            right = corner_diag[pl.ds(2 + upper, 1), :] * got[B_CORN + 4 + c : B_CORN + 5 + c, :]
            beside = beyond + row_pair(first, left, right) + z_pair(first)
            fix[c, pl.ds(at, 32), :] = first * THIRD + d_edge * beside
            fix[c, pl.ds(inner, 32), :] = d_inner * first
    high, low = split(jnp.concatenate([fix[c] for c in range(3)], axis=1))

    def finish(base, sel, table_h, table_l):
        rows = dot(sel[...], high) + dot(sel[...], low)
        total = None
        for k in range(4):
            at = slice(64 * k, 64 * k + 64)
            placed = [base[c, at, :] + rows[at, 128 * c : 128 * c + 128] for c in range(3)]
            p_high, p_low = split(jnp.concatenate(placed, axis=0))
            product = dot_t(p_high, table_h[k]) + dot_t(p_low, table_h[k]) + dot_t(p_high, table_l[k])
            total = product if total is None else total + product
        for s in range(4):
            for c in range(3):
                out[s, 16 * c : 16 * c + 16, :] = total[64 * c + 16 * s : 64 * c + 16 * s + 16, :]

    early = goes_early()

    @pl.when(early)
    def _():
        finish(*early_set)

    @pl.when(jnp.logical_not(early))
    def _():
        finish(*late_set)


def collect(early_state, late_state, fix, got, codes, out, result, sems):
    total = codes[0:1, :]
    rows = jnp.concatenate(
        [
            jnp.concatenate([got[d, 16 * c : 16 * c + 16, :] for d in range(4)], axis=0)
            for c in range(3)
        ],
        axis=1,
    )
    high, low = split(rows)
    place = lax.broadcasted_iota(jnp.int32, (128, 64), 0)

    def finish(state):
        copies = []
        for q in range(4):
            picked = jnp.where(total[:, 0:64] == (place + q * 128).astype(F32), 1.0, 0.0).astype(BF16)
            added = dot(picked, high) + dot(picked, low)
            for c in range(3):
                at = slice(q * 128, q * 128 + 128)
                final = state[c, at, :] + added[:, c * 128 : c * 128 + 128]
                if q == 0:
                    final = jnp.concatenate([final[0:64] + fix[c, 0:64, :], final[64:128]], axis=0)
                if q == 3:
                    final = jnp.concatenate([final[0:64], final[64:128] + fix[c, 64:128, :]], axis=0)
                result[c, at, :] = final
                copy = pltpu.make_async_copy(result.at[c, at, :], out.at[c, at, :], sems.at[len(copies)])
                copy.start()
                copies.append(copy)
        for copy in copies:
            copy.wait()

    early = goes_early()

    @pl.when(early)
    def _():
        finish(early_state)

    @pl.when(jnp.logical_not(early))
    def _():
        finish(late_state)


def stay(array):
    return pltpu.with_memory_space_constraint(array, pltpu.HBM)


def shape(*dims, kind=F32):
    return jax.ShapeDtypeStruct(dims, kind)


def call(body, outs, ins, scratch=(), aliases=None, to=VMEM, flops=1_000_000, moved=1_000_000, limit=16384):
    many = isinstance(outs, list)
    return pl.pallas_call(
        body,
        out_shape=outs,
        in_specs=ins,
        out_specs=[to] * len(outs) if many else to,
        scratch_shapes=list(scratch),
        input_output_aliases=aliases or {},
        cost_estimate=pl.CostEstimate(flops=flops, bytes_accessed=moved, transcendentals=0),
        compiler_params=pltpu.CompilerParams(vmem_limit_bytes=limit << 10),
    )


def local(field, source, mass, interp, parents, children, kinds, counts):
    whole = field.shape
    send, codes, field, mass = call(
        pack,
        [shape(4, A_ROWS, 128), shape(24, 128), shape(3, 512, 128), shape(512, 128)],
        [HBM] * 7,
        [
            pltpu.VMEM((2, 3, 16, 128), F32),
            pltpu.SMEM(parents.shape, jnp.int32),
            pltpu.SMEM(counts.shape, jnp.int32),
            pltpu.VMEM(parents.shape, jnp.int32),
            pltpu.VMEM(parents.shape, jnp.int32),
            pltpu.VMEM(parents.shape, jnp.int32),
            pltpu.VMEM((120, 128), F32),
            pltpu.SemaphoreType.DMA((11,)),
        ],
    )(*map(stay, (field.reshape(3, 512, 128), source, mass.reshape(512, 128), parents, counts, children, kinds)))
    source = source.reshape(3, 512, 128)
    got = lax.all_to_all(send, "group", 0, 0, tiled=True)
    pay1, pay2, rim, rim_diag, corner_diag, y_high, y_low = call(
        border,
        [
            shape(B_ROWS, 128),
            shape(B_ROWS, 128),
            shape(3, 128, 128),
            shape(128, 128),
            shape(8, 128),
            shape(256, 384, kind=BF16),
            shape(256, 384, kind=BF16),
        ],
        [VMEM] * 6,
        [pltpu.VMEM((2, 8, 128), F32)],
    )(got, field, source, mass, interp, codes)

    def smoothed(early, *pay):
        return call(
            functools.partial(smooth, early),
            [
                shape(3, 512, 128),
                shape(3, 256, 128),
                shape(256, 128, kind=BF16),
                shape(4, 128, 128, kind=BF16),
                shape(4, 128, 128, kind=BF16),
                *(shape(*p.shape) for p in pay),
            ],
            [VMEM] * 8 + [HBM] * 2 + [VMEM] * len(pay),
            [
                pltpu.VMEM((3, 512, 128), F32),
                pltpu.VMEM((3, 512, 128), F32),
                pltpu.VMEM((2, 3, 16, 128), F32),
                pltpu.VMEM((2, 3, 16, 128), F32),
                pltpu.VMEM((512, 128), F32),
                pltpu.SMEM(children.shape, jnp.int32),
                pltpu.SMEM(kinds.shape, jnp.int32),
                pltpu.SemaphoreType.DMA((2,)),
            ],
            flops=20_000_000,
            moved=8_000_000,
        )(got, field, source, mass, interp, y_high, y_low, codes, stay(children), stay(kinds), *pay)

    *early_set, pay2 = smoothed(True, pay2)
    count = lax.axis_size("curve")
    waiting = [i for i in range(64, count) if i % 64 < 2]
    inner_first = [(i, i ^ 1) for i in waiting]
    inner_last = [(i, i ^ 1) for i in range(count) if i not in waiting]
    outer = [(i, i + 1) for i in range(1, count - 1, 2)]
    outer = outer + [(b, a) for a, b in outer]
    got_first = lax.ppermute(pay1, "curve", inner_first)
    got2 = lax.ppermute(pay2, "curve", outer)
    got_last = lax.ppermute(pay1, "curve", inner_last)
    late_set = smoothed(False)
    fix, send = call(
        restrict, [shape(3, 128, 128), shape(4, 48, 128)], [VMEM] * 14
    )(rim, rim_diag, corner_diag, got_first, got_last, got2, *early_set[1:], *late_set[1:])
    got = lax.all_to_all(send, "group", 0, 0, tiled=True)
    out = call(
        collect,
        shape(3, 512, 128),
        [VMEM] * 5,
        [pltpu.VMEM((3, 512, 128), F32), pltpu.SemaphoreType.DMA((12,))],
        to=HBM,
    )(early_set[0], late_set[0], fix, got, codes)
    return out.reshape(whole)


def solution(mesh):
    in_specs = (
        P(None, "curve", "group", None),
        P(None, "curve", "group", None),
        P("curve", "group", None),
        P(),
        P("curve", "group", None, None),
        P("curve", "group", None, None),
        P("curve", "group", None, None),
        P("curve", "group", None),
    )
    out_specs = P(None, "curve", "group", None)
    return jax.shard_map(local, mesh=mesh, in_specs=in_specs, out_specs=out_specs, check_vma=False)
```

```python
import functools

import jax
import jax.numpy as jnp
from jax import lax
from jax.experimental import pallas as pl
from jax.experimental.pallas import tpu as pltpu
from jax.sharding import PartitionSpec as P


F32 = jnp.float32
BF16 = jnp.bfloat16
OMEGA = 2.0 / 3.0
THIRD = 1.0 / 3.0

PICK = 32
A_EDGE = 3 * PICK
A_PART = A_EDGE + 48
A_DIAG = A_PART + 48
A_CODE = A_DIAG + 16
A_ROWS = A_CODE + 8
B_PART = 96
B_DIAG = 192
B_CORN = 224
B_ROWS = 232

VMEM = pl.BlockSpec(memory_space=pltpu.VMEM)
SMEM = pl.BlockSpec(memory_space=pltpu.SMEM)
HBM = pl.BlockSpec(memory_space=pltpu.HBM)


def z_pair(a):
    lane = lax.broadcasted_iota(jnp.int32, a.shape, a.ndim - 1)
    low = jnp.where(lane == 0, 0.0, pltpu.roll(a, 1, a.ndim - 1))
    high = jnp.where(lane == 127, 0.0, pltpu.roll(a, 127, a.ndim - 1))
    return low + high


def row_pair(a, before, after):
    n = a.shape[0]
    row = lax.broadcasted_iota(jnp.int32, a.shape, 0)
    low = jnp.where(row == 0, before, pltpu.roll(a, 1, 0))
    high = jnp.where(row == n - 1, after, pltpu.roll(a, n - 1, 0))
    return low + high


def split(a):
    high = a.astype(BF16)
    return high, (a - high.astype(F32)).astype(BF16)


def dot(a, b):
    return jnp.dot(a, b, preferred_element_type=F32)


def dot_t(a, b):
    return lax.dot_general(a, b, (((1,), (1,)), ((), ())), preferred_element_type=F32)


def filled_group(counts):
    target = jnp.int32(0)
    for d in range(1, 4):
        target = jnp.where(counts[0, 0, d] == 16, d, target)
    return target


def column(ref, c, y):
    return ref[c, pl.ds(y, 16, stride=32), :]


def pack(
    field, source, mass, parents, counts, children, kinds, out, codes, f_all, m_all,
    s_edge, p_scalar, c_scalar, p_lane, child, kind, rows, sems,
):
    copies = [
        pltpu.make_async_copy(parents, p_scalar, sems.at[0]),
        pltpu.make_async_copy(counts, c_scalar, sems.at[1]),
        pltpu.make_async_copy(children, child, sems.at[2]),
        pltpu.make_async_copy(kinds, kind, sems.at[3]),
        pltpu.make_async_copy(parents, p_lane, sems.at[4]),
    ]
    for part in range(12):
        at = (part // 4, slice(part % 4 * 128, part % 4 * 128 + 128))
        copies.append(pltpu.make_async_copy(field.at[at], f_all.at[at], sems.at[5 + part]))
    copies = copies + [
        pltpu.make_async_copy(source.at[:, :, 0, :], s_edge.at[0], sems.at[17]),
        pltpu.make_async_copy(source.at[:, :, 31, :], s_edge.at[1], sems.at[18]),
        pltpu.make_async_copy(mass, m_all, sems.at[19]),
    ]
    for copy in copies:
        copy.start()
    g = lax.axis_index("group")
    for copy in copies[:5]:
        copy.wait()
    target = filled_group(c_scalar)
    slots = lax.broadcasted_iota(jnp.int32, (1, 16), 1)
    codes[...] = jnp.zeros((24, 128), F32)
    for d in range(4):
        codes[d : d + 1, 0:16] = jnp.where(slots < c_scalar[0, 0, d], p_lane[0, 0, d : d + 1, :], -1).astype(F32)
    codes[8:12, 0:16] = (kind[0, 0] * 512 + child[0, 0]).astype(F32)
    for at in (0, 8):
        codes[at : at + 1, :] = lane_codes(codes.at[at : at + 8, :])
    codes[16:24, :] = jnp.full((8, 128), target.astype(F32))
    for copy in copies[5:17]:
        copy.wait()
    for d in range(5):
        for k in range(8):
            p = p_scalar[0, 0, d, k] if d < 4 else p_scalar[0, 0, target, 8 + k]
            for c in range(3):
                j = c * 40 + d * 8 + k
                rows[j : j + 1, :] = f_all[c, pl.ds(p, 1), :]
    slot = lax.broadcasted_iota(jnp.int32, (8, 128), 0)
    for d in range(5):
        live = slot < c_scalar[0, 0, d] if d < 4 else slot + 8 < c_scalar[0, 0, target]
        for c in range(3):
            at = c * 40 + d * 8
            part = jnp.where(live, rows[at : at + 8, :], 0.0)
            for p in range(4):
                near = 3 if d == 4 else d - p + 1
                if 0 <= near < 4 and (d == 4 or near < 3):
                    out[p, c * PICK + near * 8 : c * PICK + near * 8 + 8, :] = part
    for copy in copies[17:]:
        copy.wait()
    block = child[0, 0]
    y = block & 31
    x = block >> 5
    sides = []
    for side, edge, inner, depth in ((0, 0, 1, y), (1, 31, 30, 31 - y)):
        diag = OMEGA / (6.0 + m_all[pl.ds(edge, 16, stride=32), :])
        firsts, parts = [], []
        for c in range(3):
            first = column(f_all, c, edge)
            beside = column(f_all, c, inner) + row_pair(first, 0.0, 0.0) + z_pair(first)
            firsts.append(first)
            parts.append(first * THIRD + diag * (s_edge[side, c] + beside))
        code = jnp.where(depth < 2, kind[0, 0] * 32 + depth * 16 + x, -1)
        sides.append((firsts, parts, diag, code.astype(F32)))
    for p in range(4):
        right = p == g + 1
        for c in range(3):
            at = A_EDGE + 16 * c
            out[p, at : at + 16, :] = jnp.where(right, sides[1][0][c], sides[0][0][c])
            at = A_PART + 16 * c
            out[p, at : at + 16, :] = jnp.where(right, sides[1][1][c], sides[0][1][c])
        out[p, A_DIAG : A_DIAG + 16, :] = jnp.where(right, sides[1][2], sides[0][2])
        out[p, A_CODE : A_CODE + 8, :] = jnp.zeros((8, 128), F32)
        out[p, A_CODE : A_CODE + 4, 0:16] = jnp.where(right, sides[1][3], sides[0][3])


def lane_codes(rows):
    total = rows[0:1, :]
    for s in range(1, 4):
        total = total + pltpu.roll(rows[s : s + 1, :], 16 * s, 1)
    return total + pltpu.roll(total, 64, 1)


def selection(codes, start, count, stride):
    place = lax.broadcasted_iota(jnp.int32, (count, 128), 0) + start
    half = lax.broadcasted_iota(jnp.int32, (count, 128), 1) >> 6
    picked = []
    for pair in range(2):
        wanted = (place + (half + 2 * pair) * stride).astype(F32)
        picked.append(jnp.where(codes == wanted, 1.0, 0.0).astype(BF16))
    return jnp.concatenate(picked, axis=1)


def edge_selection(codes):
    place = lax.broadcasted_iota(jnp.int32, (128, 128), 0)
    place = place + jnp.where(place >= 64, 384, 0)
    half = lax.broadcasted_iota(jnp.int32, (128, 128), 1) >> 6
    picked = []
    for pair in range(2):
        wanted = (place + (half + 2 * pair) * 512).astype(F32)
        picked.append(jnp.where(codes == wanted, 1.0, 0.0).T)
    picked = jnp.concatenate(picked, axis=0).astype(BF16)
    return jnp.concatenate([picked, picked], axis=1)


def slot_rows(got, near, target, d):
    rows = []
    for c in range(3):
        for s in range(4):
            rows.append(got[s, c * PICK + near * 8 : c * PICK + near * 8 + 8, :])
            more = got[s, c * PICK + 24 : c * PICK + 32, :]
            rows.append(jnp.where(target == d.astype(F32), more, 0.0))
    return jnp.concatenate(rows, axis=0)


def times(rows, table_h, table_l):
    high, low = split(rows)
    return dot(high, table_h) + dot(low, table_h) + dot(high, table_l)


def arranged(product):
    blocks = [
        [product[64 * c : 64 * c + 64, 128 * k : 128 * k + 128] for c in range(3)] for k in range(4)
    ]
    return split(jnp.concatenate([jnp.concatenate(b, axis=1) for b in blocks], axis=0))


def stacked(interp):
    return split(jnp.concatenate([interp[k] for k in range(4)], axis=1))


def neighbour(g, side):
    other = g - 1 if side == 0 else g + 1
    return (other >= 0) & (other < 4), jnp.clip(other, 0, 3)


def border(
    got, field, source, mass, interp, codes,
    pay1, pay2, rim, rim_diag, corner_diag, y_high, y_low, corners,
):
    g = lax.axis_index("group")
    odd = lax.axis_index("curve") & 1
    target = codes[16:24, :]
    table_h, table_l = stacked(interp)
    own = codes[8:9, :]
    line = lax.broadcasted_iota(jnp.int32, (8, 128), 0)
    wanted = ((line >> 1) * 32 + (line & 1) * 15).astype(F32)
    parts = [slot_rows(got, 1, target, g)]
    for side in range(2):
        _, s = neighbour(g, side)
        theirs = lane_codes(got.at[s, A_CODE : A_CODE + 8, :])
        chosen = jnp.where(theirs == wanted, 1.0, 0.0).astype(BF16)
        rows = slot_rows(got, 2 * side, target, s)
        both = split(jnp.concatenate([rows[64 * c : 64 * c + 64] for c in range(3)], axis=1))
        merged = dot(chosen, jnp.concatenate(both, axis=0))
        parts += [merged[:, 128 * c : 128 * c + 128] for c in range(3)]
    product = times(jnp.concatenate(parts, axis=0), table_h, table_l)
    high, low = arranged(product[0:192])
    y_high[...] = high
    y_low[...] = low
    chosen = jnp.concatenate([selection(own, 0, 64, 512), selection(own, 448, 64, 512)], axis=0)
    added = dot(chosen, high) + dot(chosen, low)
    for end, start in ((0, 0), (64, 448)):
        rim_diag[end : end + 64, :] = OMEGA / (6.0 + mass[start : start + 64, :])
        for c in range(3):
            more = added[end : end + 64, c * 128 : c * 128 + 128]
            rim[c, end : end + 64, :] = field[c, start : start + 64, :] + more

    corner_diag[...] = jnp.zeros((8, 128), F32)
    corners[...] = jnp.zeros((2, 8, 128), F32)
    for side in range(2):
        exists, s = neighbour(g, side)
        for end in range(2):
            x = 15 * end
            at = 2 * side + end
            corner_diag[at : at + 1, :] = jnp.where(exists, got[s, A_DIAG + x : A_DIAG + x + 1, :], 0.0)
            for c in range(3):
                value = got[s, A_EDGE + 16 * c + x : A_EDGE + 16 * c + x + 1, :]
                for k in range(4):
                    line_at = 192 + 24 * side + 8 * c + 2 * k + end
                    value = value + product[line_at : line_at + 1, 128 * k : 128 * k + 128]
                corners[end, 4 * side + c : 4 * side + c + 1, :] = jnp.where(exists, value, 0.0)

    for pay, upper in ((pay1, 1 - odd), (pay2, odd)):
        at = pl.multiple_of(upper * 96, 32)
        inner = pl.multiple_of(upper * 32 + 32, 32)
        whole = pl.multiple_of(upper * 480, 32)
        diag = rim_diag[pl.ds(at, 32), :]
        pay[B_DIAG : B_DIAG + 32, :] = diag
        pay[B_CORN : B_CORN + 8, :] = corners[upper]
        for c in range(3):
            first = rim[c, pl.ds(at, 32), :]
            left = corners[upper, c : c + 1, :]
            right = corners[upper, 4 + c : 5 + c, :]
            beside = rim[c, pl.ds(inner, 32), :] + row_pair(first, left, right) + z_pair(first)
            pay[32 * c : 32 * c + 32, :] = first
            pay[B_PART + 32 * c : B_PART + 32 * c + 32, :] = first * THIRD + diag * (
                source[c, pl.ds(whole, 32), :] + beside
            )


def waits():
    c = lax.axis_index("curve")
    return (c >= 64) & (c % 64 < 2)


def goes_early():
    c = lax.axis_index("curve")
    return ((c % 64 == 0) & (c > 0)) | (c % 64 == 1)


def smooth(early, got, field, source, mass, interp, y_high, y_low, codes, children, kinds, *rest):
    if early:
        pay, *rest = rest
        state, base, sel, table_h, table_l, passed, cst, mid, near, sweep, diag, child, kind, sems = rest
        passed[...] = pay[...]
    else:
        state, base, sel, table_h, table_l, cst, mid, near, sweep, diag, child, kind, sems = rest

    @pl.when(goes_early() == early)
    def _():
        copies = [
            pltpu.make_async_copy(children, child, sems.at[0]),
            pltpu.make_async_copy(kinds, kind, sems.at[1]),
        ]
        for copy in copies:
            copy.start()
        g = lax.axis_index("group")
        target = codes[16:24, :]
        stack_h, stack_l = stacked(interp)
        table_h[...] = stack_h
        table_l[...] = stack_l
        own = codes[8:9, :]
        sel[...] = edge_selection(own)
        for q in range(4):
            chosen = selection(own, q * 128, 128, 512)
            added = dot(chosen, y_high[...]) + dot(chosen, y_low[...])
            rows = slice(q * 128, q * 128 + 128)
            diag[rows, :] = OMEGA / (6.0 + mass[rows, :])
            for c in range(3):
                cst[c, rows, :] = field[c, rows, :] + added[:, c * 128 : c * 128 + 128]

        for side in range(2):
            exists, s = neighbour(g, side)
            high, low = arranged(times(slot_rows(got, 2 * side, target, s), stack_h, stack_l))
            chosen = selection(lane_codes(got.at[s, A_CODE : A_CODE + 8, :]), 0, 32, 32)
            added = dot(chosen, high) + dot(chosen, low)
            beyond = got[s, A_DIAG : A_DIAG + 16, :]
            for c in range(3):
                first = added[0:16, c * 128 : c * 128 + 128]
                second = added[16:32, c * 128 : c * 128 + 128]
                edge = got[s, A_EDGE + 16 * c : A_EDGE + 16 * c + 16, :] + first
                near[side, c] = jnp.where(exists, edge, 0.0)
                beside = second + row_pair(first, 0.0, 0.0) + z_pair(first)
                beside = beside + column(cst, c, 0 if side == 0 else 31)
                part = got[s, A_PART + 16 * c : A_PART + 16 * c + 16, :] + first * THIRD
                sweep[side, c] = jnp.where(exists, part + beyond * beside, 0.0)

        def step(before, halo, result):
            for x in range(16):
                rows = slice(32 * x, 32 * x + 32)
                d = diag[rows, :]
                for c in range(3):
                    centre = before[c, rows, :]
                    beside = row_pair(centre, halo[0, c, x : x + 1, :], halo[1, c, x : x + 1, :]) + z_pair(centre)
                    if x > 0:
                        beside = beside + before[c, 32 * x - 32 : 32 * x, :]
                    if x < 15:
                        beside = beside + before[c, 32 * x + 32 : 32 * x + 64, :]
                    result[c, rows, :] = centre * THIRD + d * (source[c, rows, :] + beside)

        step(cst, near, mid)
        step(mid, sweep, state)
        base[...] = jnp.zeros(base.shape, F32)
        for copy in copies:
            copy.wait()
        for s in range(4):
            for k in range(16):
                b = child[0, 0, s, k]
                row = kind[0, 0, s, k] * 64 + (s * 16 + k)
                for c in range(3):
                    base[c, pl.ds(row, 1), :] = state[c, pl.ds(b, 1), :] - cst[c, pl.ds(b, 1), :]


def restrict(rim, rim_diag, corner_diag, got_first, got_last, got2, *rest):
    early_set, late_set, (fix, out) = rest[:4], rest[4:8], rest[8:]
    odd = lax.axis_index("curve") & 1
    got1 = jnp.where(waits(), got_first[...], got_last[...])
    for got, upper in ((got1, 1 - odd), (got2[...], odd)):
        at = pl.multiple_of(upper * 96, 32)
        inner = pl.multiple_of(upper * 32 + 32, 32)
        d_edge = rim_diag[pl.ds(at, 32), :]
        d_inner = rim_diag[pl.ds(inner, 32), :]
        far = got[B_DIAG : B_DIAG + 32, :]
        for c in range(3):
            beyond = got[B_PART + 32 * c : B_PART + 32 * c + 32, :] + far * rim[c, pl.ds(at, 32), :]
            first = d_edge * got[32 * c : 32 * c + 32, :]
            left = corner_diag[pl.ds(upper, 1), :] * got[B_CORN + c : B_CORN + c + 1, :]
            right = corner_diag[pl.ds(2 + upper, 1), :] * got[B_CORN + 4 + c : B_CORN + 5 + c, :]
            beside = beyond + row_pair(first, left, right) + z_pair(first)
            fix[c, pl.ds(at, 32), :] = first * THIRD + d_edge * beside
            fix[c, pl.ds(inner, 32), :] = d_inner * first
    both = jnp.concatenate(split(jnp.concatenate([fix[c] for c in range(3)], axis=1)), axis=0)

    def finish(base, sel, table_h, table_l):
        rows = dot(sel[...], both)
        placed = []
        for k in range(4):
            at = slice(64 * k, 64 * k + 64)
            blocks = [base[c, at, :] + rows[at, 128 * c : 128 * c + 128] for c in range(3)]
            placed.append(jnp.concatenate(blocks, axis=0))
        high, low = split(jnp.concatenate(placed, axis=1))
        total = dot_t(high, table_h[...]) + dot_t(low, table_h[...]) + dot_t(high, table_l[...])
        for s in range(4):
            for c in range(3):
                out[s, 16 * c : 16 * c + 16, :] = total[64 * c + 16 * s : 64 * c + 16 * s + 16, :]

    early = goes_early()

    @pl.when(early)
    def _():
        finish(*early_set)

    @pl.when(jnp.logical_not(early))
    def _():
        finish(*late_set)


def collect(early_state, late_state, fix, got, codes, out, result, sems):
    total = codes[0:1, :]
    rows = jnp.concatenate(
        [
            jnp.concatenate([got[d, 16 * c : 16 * c + 16, :] for d in range(4)], axis=0)
            for c in range(3)
        ],
        axis=1,
    )
    both = jnp.concatenate(split(rows), axis=0)
    place = lax.broadcasted_iota(jnp.int32, (128, 128), 0)

    def finish(state):
        copies = []
        for q in range(4):
            picked = jnp.where(total == (place + q * 128).astype(F32), 1.0, 0.0).astype(BF16)
            added = dot(picked, both)
            for c in range(3):
                at = slice(q * 128, q * 128 + 128)
                final = state[c, at, :] + added[:, c * 128 : c * 128 + 128]
                if q == 0:
                    final = jnp.concatenate([final[0:64] + fix[c, 0:64, :], final[64:128]], axis=0)
                if q == 3:
                    final = jnp.concatenate([final[0:64], final[64:128] + fix[c, 64:128, :]], axis=0)
                result[c, at, :] = final
                copy = pltpu.make_async_copy(result.at[c, at, :], out.at[c, at, :], sems.at[len(copies)])
                copy.start()
                copies.append(copy)
        for copy in copies:
            copy.wait()

    early = goes_early()

    @pl.when(early)
    def _():
        finish(early_state)

    @pl.when(jnp.logical_not(early))
    def _():
        finish(late_state)


def stay(array):
    return pltpu.with_memory_space_constraint(array, pltpu.HBM)


def shape(*dims, kind=F32):
    return jax.ShapeDtypeStruct(dims, kind)


def call(body, outs, ins, scratch=(), aliases=None, to=VMEM, flops=1_000_000, moved=1_000_000, limit=16384):
    many = isinstance(outs, list)
    return pl.pallas_call(
        body,
        out_shape=outs,
        in_specs=ins,
        out_specs=[to] * len(outs) if many else to,
        scratch_shapes=list(scratch),
        input_output_aliases=aliases or {},
        cost_estimate=pl.CostEstimate(flops=flops, bytes_accessed=moved, transcendentals=0),
        compiler_params=pltpu.CompilerParams(vmem_limit_bytes=limit << 10),
    )


def local(field, source, mass, interp, parents, children, kinds, counts):
    whole = field.shape
    send, codes, field, mass = call(
        pack,
        [shape(4, A_ROWS, 128), shape(24, 128), shape(3, 512, 128), shape(512, 128)],
        [HBM] * 7,
        [
            pltpu.VMEM((2, 3, 16, 128), F32),
            pltpu.SMEM(parents.shape, jnp.int32),
            pltpu.SMEM(counts.shape, jnp.int32),
            pltpu.VMEM(parents.shape, jnp.int32),
            pltpu.VMEM(parents.shape, jnp.int32),
            pltpu.VMEM(parents.shape, jnp.int32),
            pltpu.VMEM((120, 128), F32),
            pltpu.SemaphoreType.DMA((20,)),
        ],
    )(*map(stay, (field.reshape(3, 512, 128), source, mass.reshape(512, 128), parents, counts, children, kinds)))
    source = source.reshape(3, 512, 128)
    got = lax.all_to_all(send, "group", 0, 0, tiled=True)
    pay1, pay2, rim, rim_diag, corner_diag, y_high, y_low = call(
        border,
        [
            shape(B_ROWS, 128),
            shape(B_ROWS, 128),
            shape(3, 128, 128),
            shape(128, 128),
            shape(8, 128),
            shape(256, 384, kind=BF16),
            shape(256, 384, kind=BF16),
        ],
        [VMEM] * 6,
        [pltpu.VMEM((2, 8, 128), F32)],
    )(got, field, source, mass, interp, codes)

    def smoothed(early, *pay):
        return call(
            functools.partial(smooth, early),
            [
                shape(3, 512, 128),
                shape(3, 256, 128),
                shape(256, 256, kind=BF16),
                shape(128, 512, kind=BF16),
                shape(128, 512, kind=BF16),
                *(shape(*p.shape) for p in pay),
            ],
            [VMEM] * 8 + [HBM] * 2 + [VMEM] * len(pay),
            [
                pltpu.VMEM((3, 512, 128), F32),
                pltpu.VMEM((3, 512, 128), F32),
                pltpu.VMEM((2, 3, 16, 128), F32),
                pltpu.VMEM((2, 3, 16, 128), F32),
                pltpu.VMEM((512, 128), F32),
                pltpu.SMEM(children.shape, jnp.int32),
                pltpu.SMEM(kinds.shape, jnp.int32),
                pltpu.SemaphoreType.DMA((2,)),
            ],
            flops=20_000_000,
            moved=8_000_000,
        )(got, field, source, mass, interp, y_high, y_low, codes, stay(children), stay(kinds), *pay)

    *early_set, pay2 = smoothed(True, pay2)
    count = lax.axis_size("curve")
    waiting = [i for i in range(64, count) if i % 64 < 2]
    inner_first = [(i, i ^ 1) for i in waiting]
    inner_last = [(i, i ^ 1) for i in range(count) if i not in waiting]
    outer = [(i, i + 1) for i in range(1, count - 1, 2)]
    outer = outer + [(b, a) for a, b in outer]
    got_first = lax.ppermute(pay1, "curve", inner_first)
    got2 = lax.ppermute(pay2, "curve", outer)
    got_last = lax.ppermute(pay1, "curve", inner_last)
    late_set = smoothed(False)
    fix, send = call(
        restrict, [shape(3, 128, 128), shape(4, 48, 128)], [VMEM] * 14
    )(rim, rim_diag, corner_diag, got_first, got_last, got2, *early_set[1:], *late_set[1:])
    got = lax.all_to_all(send, "group", 0, 0, tiled=True)
    out = call(
        collect,
        shape(3, 512, 128),
        [VMEM] * 5,
        [pltpu.VMEM((3, 512, 128), F32), pltpu.SemaphoreType.DMA((12,))],
        to=HBM,
    )(early_set[0], late_set[0], fix, got, codes)
    return out.reshape(whole)


def solution(mesh):
    in_specs = (
        P(None, "curve", "group", None),
        P(None, "curve", "group", None),
        P("curve", "group", None),
        P(),
        P("curve", "group", None, None),
        P("curve", "group", None, None),
        P("curve", "group", None, None),
        P("curve", "group", None),
    )
    out_specs = P(None, "curve", "group", None)
    return jax.shard_map(local, mesh=mesh, in_specs=in_specs, out_specs=out_specs, check_vma=False)
```

```python
import functools

import jax
import jax.numpy as jnp
from jax import lax
from jax.experimental import pallas as pl
from jax.experimental.pallas import tpu as pltpu
from jax.sharding import PartitionSpec as P


F32 = jnp.float32
BF16 = jnp.bfloat16
OMEGA = 2.0 / 3.0
THIRD = 1.0 / 3.0

PICK = 32
A_EDGE = 3 * PICK
A_PART = A_EDGE + 48
A_DIAG = A_PART + 48
A_CODE = A_DIAG + 16
A_ROWS = A_CODE + 8
B_PART = 96
B_DIAG = 192
B_CORN = 224
B_ROWS = 232

VMEM = pl.BlockSpec(memory_space=pltpu.VMEM)
SMEM = pl.BlockSpec(memory_space=pltpu.SMEM)
HBM = pl.BlockSpec(memory_space=pltpu.HBM)


def z_pair(a):
    lane = lax.broadcasted_iota(jnp.int32, a.shape, a.ndim - 1)
    low = jnp.where(lane == 0, 0.0, pltpu.roll(a, 1, a.ndim - 1))
    high = jnp.where(lane == 127, 0.0, pltpu.roll(a, 127, a.ndim - 1))
    return low + high


def row_pair(a, before, after):
    n = a.shape[0]
    row = lax.broadcasted_iota(jnp.int32, a.shape, 0)
    low = jnp.where(row == 0, before, pltpu.roll(a, 1, 0))
    high = jnp.where(row == n - 1, after, pltpu.roll(a, n - 1, 0))
    return low + high


def split(a):
    high = a.astype(BF16)
    return high, (a - high.astype(F32)).astype(BF16)


def dot(a, b):
    return jnp.dot(a, b, preferred_element_type=F32)


def dot_t(a, b):
    return lax.dot_general(a, b, (((1,), (1,)), ((), ())), preferred_element_type=F32)


def filled_group(counts):
    target = jnp.int32(0)
    for d in range(1, 4):
        target = jnp.where(counts[0, 0, d] == 16, d, target)
    return target


def column(ref, c, y):
    return ref[c, pl.ds(y, 16, stride=32), :]


def pack(
    field, source, mass, parents, counts, children, kinds, out, codes, f_all, m_all,
    s_edge, p_scalar, c_scalar, p_lane, child, kind, rows, sems,
):
    copies = [
        pltpu.make_async_copy(parents, p_scalar, sems.at[0]),
        pltpu.make_async_copy(counts, c_scalar, sems.at[1]),
        pltpu.make_async_copy(children, child, sems.at[2]),
        pltpu.make_async_copy(kinds, kind, sems.at[3]),
        pltpu.make_async_copy(parents, p_lane, sems.at[4]),
    ]
    for c in range(3):
        copies.append(pltpu.make_async_copy(field.at[c], f_all.at[c], sems.at[5 + c]))
    copies = copies + [
        pltpu.make_async_copy(source.at[:, :, 0, :], s_edge.at[0], sems.at[8]),
        pltpu.make_async_copy(source.at[:, :, 31, :], s_edge.at[1], sems.at[9]),
        pltpu.make_async_copy(mass, m_all, sems.at[10]),
    ]
    for copy in copies:
        copy.start()
    g = lax.axis_index("group")
    for copy in copies[:5]:
        copy.wait()
    target = filled_group(c_scalar)
    slots = lax.broadcasted_iota(jnp.int32, (1, 16), 1)
    codes[...] = jnp.zeros((24, 128), F32)
    for d in range(4):
        codes[d : d + 1, 0:16] = jnp.where(slots < c_scalar[0, 0, d], p_lane[0, 0, d : d + 1, :], -1).astype(F32)
    codes[8:12, 0:16] = (kind[0, 0] * 512 + child[0, 0]).astype(F32)
    for at in (0, 8):
        codes[at : at + 1, :] = lane_codes(codes.at[at : at + 8, :])
    codes[16:24, :] = jnp.full((8, 128), target.astype(F32))
    for c in range(3):
        copies[5 + c].wait()
        for d in range(5):
            for k in range(8):
                p = p_scalar[0, 0, d, k] if d < 4 else p_scalar[0, 0, target, 8 + k]
                j = c * 40 + d * 8 + k
                rows[j : j + 1, :] = f_all[c, pl.ds(p, 1), :]
    slot = lax.broadcasted_iota(jnp.int32, (8, 128), 0)
    for d in range(5):
        live = slot < c_scalar[0, 0, d] if d < 4 else slot + 8 < c_scalar[0, 0, target]
        for c in range(3):
            at = c * 40 + d * 8
            part = jnp.where(live, rows[at : at + 8, :], 0.0)
            for p in range(4):
                near = 3 if d == 4 else d - p + 1
                if 0 <= near < 4 and (d == 4 or near < 3):
                    out[p, c * PICK + near * 8 : c * PICK + near * 8 + 8, :] = part
    for copy in copies[8:]:
        copy.wait()
    block = child[0, 0]
    y = block & 31
    x = block >> 5
    sides = []
    for side, edge, inner, depth in ((0, 0, 1, y), (1, 31, 30, 31 - y)):
        diag = OMEGA / (6.0 + m_all[pl.ds(edge, 16, stride=32), :])
        firsts, parts = [], []
        for c in range(3):
            first = column(f_all, c, edge)
            beside = column(f_all, c, inner) + row_pair(first, 0.0, 0.0) + z_pair(first)
            firsts.append(first)
            parts.append(first * THIRD + diag * (s_edge[side, c] + beside))
        code = jnp.where(depth < 2, kind[0, 0] * 32 + depth * 16 + x, -1)
        sides.append((firsts, parts, diag, code.astype(F32)))
    for p in range(4):
        right = p == g + 1
        for c in range(3):
            at = A_EDGE + 16 * c
            out[p, at : at + 16, :] = jnp.where(right, sides[1][0][c], sides[0][0][c])
            at = A_PART + 16 * c
            out[p, at : at + 16, :] = jnp.where(right, sides[1][1][c], sides[0][1][c])
        out[p, A_DIAG : A_DIAG + 16, :] = jnp.where(right, sides[1][2], sides[0][2])
        out[p, A_CODE : A_CODE + 8, :] = jnp.zeros((8, 128), F32)
        out[p, A_CODE : A_CODE + 4, 0:16] = jnp.where(right, sides[1][3], sides[0][3])


def lane_codes(rows):
    total = rows[0:1, :]
    for s in range(1, 4):
        total = total + pltpu.roll(rows[s : s + 1, :], 16 * s, 1)
    return total + pltpu.roll(total, 64, 1)


def selection(codes, start, count, stride):
    place = lax.broadcasted_iota(jnp.int32, (count, 128), 0) + start
    half = lax.broadcasted_iota(jnp.int32, (count, 128), 1) >> 6
    picked = []
    for pair in range(2):
        wanted = (place + (half + 2 * pair) * stride).astype(F32)
        picked.append(jnp.where(codes == wanted, 1.0, 0.0).astype(BF16))
    return jnp.concatenate(picked, axis=1)


def edge_selection(codes):
    place = lax.broadcasted_iota(jnp.int32, (128, 128), 0)
    place = place + jnp.where(place >= 64, 384, 0)
    half = lax.broadcasted_iota(jnp.int32, (128, 128), 1) >> 6
    picked = []
    for pair in range(2):
        wanted = (place + (half + 2 * pair) * 512).astype(F32)
        picked.append(jnp.where(codes == wanted, 1.0, 0.0).T)
    picked = jnp.concatenate(picked, axis=0).astype(BF16)
    return jnp.concatenate([picked, picked], axis=1)


def slot_rows(got, near, target, d):
    rows = []
    for c in range(3):
        for s in range(4):
            rows.append(got[s, c * PICK + near * 8 : c * PICK + near * 8 + 8, :])
            more = got[s, c * PICK + 24 : c * PICK + 32, :]
            rows.append(jnp.where(target == d.astype(F32), more, 0.0))
    return jnp.concatenate(rows, axis=0)


def times(rows, table_h, table_l):
    high, low = split(rows)
    return dot(high, table_h) + dot(low, table_h) + dot(high, table_l)


def arranged(product):
    blocks = [
        [product[64 * c : 64 * c + 64, 128 * k : 128 * k + 128] for c in range(3)] for k in range(4)
    ]
    return split(jnp.concatenate([jnp.concatenate(b, axis=1) for b in blocks], axis=0))


def stacked(interp):
    return split(jnp.concatenate([interp[k] for k in range(4)], axis=1))


def neighbour(g, side):
    other = g - 1 if side == 0 else g + 1
    return (other >= 0) & (other < 4), jnp.clip(other, 0, 3)


def border(
    got, field, source, mass, interp, codes,
    pay1, pay2, rim, rim_diag, corner_diag, y_high, y_low, corners,
):
    g = lax.axis_index("group")
    odd = lax.axis_index("curve") & 1
    target = codes[16:24, :]
    table_h, table_l = stacked(interp)
    own = codes[8:9, :]
    line = lax.broadcasted_iota(jnp.int32, (8, 128), 0)
    wanted = ((line >> 1) * 32 + (line & 1) * 15).astype(F32)
    parts = [slot_rows(got, 1, target, g)]
    for side in range(2):
        _, s = neighbour(g, side)
        theirs = lane_codes(got.at[s, A_CODE : A_CODE + 8, :])
        chosen = jnp.where(theirs == wanted, 1.0, 0.0).astype(BF16)
        rows = slot_rows(got, 2 * side, target, s)
        both = split(jnp.concatenate([rows[64 * c : 64 * c + 64] for c in range(3)], axis=1))
        merged = dot(chosen, jnp.concatenate(both, axis=0))
        parts += [merged[:, 128 * c : 128 * c + 128] for c in range(3)]
    product = times(jnp.concatenate(parts, axis=0), table_h, table_l)
    high, low = arranged(product[0:192])
    y_high[...] = high
    y_low[...] = low
    chosen = jnp.concatenate([selection(own, 0, 64, 512), selection(own, 448, 64, 512)], axis=0)
    added = dot(chosen, high) + dot(chosen, low)
    for end, start in ((0, 0), (64, 448)):
        rim_diag[end : end + 64, :] = OMEGA / (6.0 + mass[start : start + 64, :])
        for c in range(3):
            more = added[end : end + 64, c * 128 : c * 128 + 128]
            rim[c, end : end + 64, :] = field[c, start : start + 64, :] + more

    corner_diag[...] = jnp.zeros((8, 128), F32)
    corners[...] = jnp.zeros((2, 8, 128), F32)
    for side in range(2):
        exists, s = neighbour(g, side)
        for end in range(2):
            x = 15 * end
            at = 2 * side + end
            corner_diag[at : at + 1, :] = jnp.where(exists, got[s, A_DIAG + x : A_DIAG + x + 1, :], 0.0)
            for c in range(3):
                value = got[s, A_EDGE + 16 * c + x : A_EDGE + 16 * c + x + 1, :]
                for k in range(4):
                    line_at = 192 + 24 * side + 8 * c + 2 * k + end
                    value = value + product[line_at : line_at + 1, 128 * k : 128 * k + 128]
                corners[end, 4 * side + c : 4 * side + c + 1, :] = jnp.where(exists, value, 0.0)

    for pay, upper in ((pay1, 1 - odd), (pay2, odd)):
        at = pl.multiple_of(upper * 96, 32)
        inner = pl.multiple_of(upper * 32 + 32, 32)
        whole = pl.multiple_of(upper * 480, 32)
        diag = rim_diag[pl.ds(at, 32), :]
        pay[B_DIAG : B_DIAG + 32, :] = diag
        pay[B_CORN : B_CORN + 8, :] = corners[upper]
        for c in range(3):
            first = rim[c, pl.ds(at, 32), :]
            left = corners[upper, c : c + 1, :]
            right = corners[upper, 4 + c : 5 + c, :]
            beside = rim[c, pl.ds(inner, 32), :] + row_pair(first, left, right) + z_pair(first)
            pay[32 * c : 32 * c + 32, :] = first
            pay[B_PART + 32 * c : B_PART + 32 * c + 32, :] = first * THIRD + diag * (
                source[c, pl.ds(whole, 32), :] + beside
            )


def waits():
    c = lax.axis_index("curve")
    return (c >= 64) & (c % 64 < 2)


def goes_early():
    c = lax.axis_index("curve")
    return ((c % 64 == 0) & (c > 0)) | (c % 64 == 1)


def smooth(early, got, field, source, mass, interp, y_high, y_low, codes, children, kinds, *rest):
    if early:
        pay, *rest = rest
        state, base, sel, table_h, table_l, passed, cst, mid, near, sweep, diag, child, kind, sems = rest
        passed[...] = pay[...]
    else:
        state, base, sel, table_h, table_l, cst, mid, near, sweep, diag, child, kind, sems = rest

    @pl.when(goes_early() == early)
    def _():
        copies = [
            pltpu.make_async_copy(children, child, sems.at[0]),
            pltpu.make_async_copy(kinds, kind, sems.at[1]),
        ]
        for copy in copies:
            copy.start()
        g = lax.axis_index("group")
        target = codes[16:24, :]
        stack_h, stack_l = stacked(interp)
        table_h[...] = stack_h
        table_l[...] = stack_l
        own = codes[8:9, :]
        sel[...] = edge_selection(own)
        for q in range(4):
            chosen = selection(own, q * 128, 128, 512)
            added = dot(chosen, y_high[...]) + dot(chosen, y_low[...])
            rows = slice(q * 128, q * 128 + 128)
            diag[rows, :] = OMEGA / (6.0 + mass[rows, :])
            for c in range(3):
                cst[c, rows, :] = field[c, rows, :] + added[:, c * 128 : c * 128 + 128]

        for side in range(2):
            exists, s = neighbour(g, side)
            high, low = arranged(times(slot_rows(got, 2 * side, target, s), stack_h, stack_l))
            chosen = selection(lane_codes(got.at[s, A_CODE : A_CODE + 8, :]), 0, 32, 32)
            added = dot(chosen, high) + dot(chosen, low)
            beyond = got[s, A_DIAG : A_DIAG + 16, :]
            for c in range(3):
                first = added[0:16, c * 128 : c * 128 + 128]
                second = added[16:32, c * 128 : c * 128 + 128]
                edge = got[s, A_EDGE + 16 * c : A_EDGE + 16 * c + 16, :] + first
                near[side, c] = jnp.where(exists, edge, 0.0)
                beside = second + row_pair(first, 0.0, 0.0) + z_pair(first)
                beside = beside + column(cst, c, 0 if side == 0 else 31)
                part = got[s, A_PART + 16 * c : A_PART + 16 * c + 16, :] + first * THIRD
                sweep[side, c] = jnp.where(exists, part + beyond * beside, 0.0)

        def step(before, halo, result):
            for x in range(16):
                rows = slice(32 * x, 32 * x + 32)
                d = diag[rows, :]
                for c in range(3):
                    centre = before[c, rows, :]
                    beside = row_pair(centre, halo[0, c, x : x + 1, :], halo[1, c, x : x + 1, :]) + z_pair(centre)
                    if x > 0:
                        beside = beside + before[c, 32 * x - 32 : 32 * x, :]
                    if x < 15:
                        beside = beside + before[c, 32 * x + 32 : 32 * x + 64, :]
                    result[c, rows, :] = centre * THIRD + d * (source[c, rows, :] + beside)

        step(cst, near, mid)
        step(mid, sweep, state)
        base[...] = jnp.zeros(base.shape, F32)
        for copy in copies:
            copy.wait()
        for s in range(4):
            for k in range(16):
                b = child[0, 0, s, k]
                row = kind[0, 0, s, k] * 64 + (s * 16 + k)
                for c in range(3):
                    base[c, pl.ds(row, 1), :] = state[c, pl.ds(b, 1), :] - cst[c, pl.ds(b, 1), :]


def restrict(rim, rim_diag, corner_diag, got_first, got_last, got_out, got_back, *rest):
    early_set, late_set, (fix, out) = rest[:4], rest[4:8], rest[8:]
    odd = lax.axis_index("curve") & 1
    got1 = jnp.where(waits(), got_first[...], got_last[...])
    got2 = jnp.where(odd == 1, got_back[...], got_out[...])
    for got, upper in ((got1, 1 - odd), (got2, odd)):
        at = pl.multiple_of(upper * 96, 32)
        inner = pl.multiple_of(upper * 32 + 32, 32)
        d_edge = rim_diag[pl.ds(at, 32), :]
        d_inner = rim_diag[pl.ds(inner, 32), :]
        far = got[B_DIAG : B_DIAG + 32, :]
        for c in range(3):
            beyond = got[B_PART + 32 * c : B_PART + 32 * c + 32, :] + far * rim[c, pl.ds(at, 32), :]
            first = d_edge * got[32 * c : 32 * c + 32, :]
            left = corner_diag[pl.ds(upper, 1), :] * got[B_CORN + c : B_CORN + c + 1, :]
            right = corner_diag[pl.ds(2 + upper, 1), :] * got[B_CORN + 4 + c : B_CORN + 5 + c, :]
            beside = beyond + row_pair(first, left, right) + z_pair(first)
            fix[c, pl.ds(at, 32), :] = first * THIRD + d_edge * beside
            fix[c, pl.ds(inner, 32), :] = d_inner * first
    both = jnp.concatenate(split(jnp.concatenate([fix[c] for c in range(3)], axis=1)), axis=0)

    def finish(base, sel, table_h, table_l):
        rows = dot(sel[...], both)
        placed = []
        for k in range(4):
            at = slice(64 * k, 64 * k + 64)
            blocks = [base[c, at, :] + rows[at, 128 * c : 128 * c + 128] for c in range(3)]
            placed.append(jnp.concatenate(blocks, axis=0))
        high, low = split(jnp.concatenate(placed, axis=1))
        total = dot_t(high, table_h[...]) + dot_t(low, table_h[...]) + dot_t(high, table_l[...])
        for s in range(4):
            for c in range(3):
                out[s, 16 * c : 16 * c + 16, :] = total[64 * c + 16 * s : 64 * c + 16 * s + 16, :]

    early = goes_early()

    @pl.when(early)
    def _():
        finish(*early_set)

    @pl.when(jnp.logical_not(early))
    def _():
        finish(*late_set)


def collect(early_state, late_state, fix, got, codes, out, result, sems):
    total = codes[0:1, :]
    rows = jnp.concatenate(
        [
            jnp.concatenate([got[d, 16 * c : 16 * c + 16, :] for d in range(4)], axis=0)
            for c in range(3)
        ],
        axis=1,
    )
    both = jnp.concatenate(split(rows), axis=0)
    place = lax.broadcasted_iota(jnp.int32, (128, 128), 0)

    def finish(state):
        copies = []
        for q in range(4):
            picked = jnp.where(total == (place + q * 128).astype(F32), 1.0, 0.0).astype(BF16)
            added = dot(picked, both)
            for c in range(3):
                at = slice(q * 128, q * 128 + 128)
                final = state[c, at, :] + added[:, c * 128 : c * 128 + 128]
                if q == 0:
                    final = jnp.concatenate([final[0:64] + fix[c, 0:64, :], final[64:128]], axis=0)
                if q == 3:
                    final = jnp.concatenate([final[0:64], final[64:128] + fix[c, 64:128, :]], axis=0)
                result[c, at, :] = final
                copy = pltpu.make_async_copy(result.at[c, at, :], out.at[c, at, :], sems.at[len(copies)])
                copy.start()
                copies.append(copy)
        for copy in copies:
            copy.wait()

    early = goes_early()

    @pl.when(early)
    def _():
        finish(early_state)

    @pl.when(jnp.logical_not(early))
    def _():
        finish(late_state)


def stay(array):
    return pltpu.with_memory_space_constraint(array, pltpu.HBM)


def shape(*dims, kind=F32):
    return jax.ShapeDtypeStruct(dims, kind)


def call(body, outs, ins, scratch=(), aliases=None, to=VMEM, flops=1_000_000, moved=1_000_000, limit=16384):
    many = isinstance(outs, list)
    return pl.pallas_call(
        body,
        out_shape=outs,
        in_specs=ins,
        out_specs=[to] * len(outs) if many else to,
        scratch_shapes=list(scratch),
        input_output_aliases=aliases or {},
        cost_estimate=pl.CostEstimate(flops=flops, bytes_accessed=moved, transcendentals=0),
        compiler_params=pltpu.CompilerParams(vmem_limit_bytes=limit << 10),
    )


def local(field, source, mass, interp, parents, children, kinds, counts):
    whole = field.shape
    send, codes, field, mass = call(
        pack,
        [shape(4, A_ROWS, 128), shape(24, 128), shape(3, 512, 128), shape(512, 128)],
        [HBM] * 7,
        [
            pltpu.VMEM((2, 3, 16, 128), F32),
            pltpu.SMEM(parents.shape, jnp.int32),
            pltpu.SMEM(counts.shape, jnp.int32),
            pltpu.VMEM(parents.shape, jnp.int32),
            pltpu.VMEM(parents.shape, jnp.int32),
            pltpu.VMEM(parents.shape, jnp.int32),
            pltpu.VMEM((120, 128), F32),
            pltpu.SemaphoreType.DMA((11,)),
        ],
    )(*map(stay, (field.reshape(3, 512, 128), source, mass.reshape(512, 128), parents, counts, children, kinds)))
    source = source.reshape(3, 512, 128)
    got = lax.all_to_all(send, "group", 0, 0, tiled=True)
    pay1, pay2, rim, rim_diag, corner_diag, y_high, y_low = call(
        border,
        [
            shape(B_ROWS, 128),
            shape(B_ROWS, 128),
            shape(3, 128, 128),
            shape(128, 128),
            shape(8, 128),
            shape(256, 384, kind=BF16),
            shape(256, 384, kind=BF16),
        ],
        [VMEM] * 6,
        [pltpu.VMEM((2, 8, 128), F32)],
    )(got, field, source, mass, interp, codes)

    def smoothed(early, *pay):
        return call(
            functools.partial(smooth, early),
            [
                shape(3, 512, 128),
                shape(3, 256, 128),
                shape(256, 256, kind=BF16),
                shape(128, 512, kind=BF16),
                shape(128, 512, kind=BF16),
                *(shape(*p.shape) for p in pay),
            ],
            [VMEM] * 8 + [HBM] * 2 + [VMEM] * len(pay),
            [
                pltpu.VMEM((3, 512, 128), F32),
                pltpu.VMEM((3, 512, 128), F32),
                pltpu.VMEM((2, 3, 16, 128), F32),
                pltpu.VMEM((2, 3, 16, 128), F32),
                pltpu.VMEM((512, 128), F32),
                pltpu.SMEM(children.shape, jnp.int32),
                pltpu.SMEM(kinds.shape, jnp.int32),
                pltpu.SemaphoreType.DMA((2,)),
            ],
            flops=20_000_000,
            moved=8_000_000,
        )(got, field, source, mass, interp, y_high, y_low, codes, stay(children), stay(kinds), *pay)

    *early_set, back = smoothed(True, pay2)
    count = lax.axis_size("curve")
    waiting = [i for i in range(64, count) if i % 64 < 2]
    inner_first = [(i, i ^ 1) for i in waiting]
    inner_last = [(i, i ^ 1) for i in range(count) if i not in waiting]
    outward = [(i, i + 1) for i in range(1, count - 1, 2)]
    got_out = lax.ppermute(pay2, "curve", outward)
    got_first = lax.ppermute(pay1, "curve", inner_first)
    got_back = lax.ppermute(back, "curve", [(b, a) for a, b in outward])
    got_last = lax.ppermute(pay1, "curve", inner_last)
    late_set = smoothed(False)
    fix, send = call(
        restrict, [shape(3, 128, 128), shape(4, 48, 128)], [VMEM] * 15
    )(rim, rim_diag, corner_diag, got_first, got_last, got_out, got_back, *early_set[1:], *late_set[1:])
    got = lax.all_to_all(send, "group", 0, 0, tiled=True)
    out = call(
        collect,
        shape(3, 512, 128),
        [VMEM] * 5,
        [pltpu.VMEM((3, 512, 128), F32), pltpu.SemaphoreType.DMA((12,))],
        to=HBM,
    )(early_set[0], late_set[0], fix, got, codes)
    return out.reshape(whole)


def solution(mesh):
    in_specs = (
        P(None, "curve", "group", None),
        P(None, "curve", "group", None),
        P("curve", "group", None),
        P(),
        P("curve", "group", None, None),
        P("curve", "group", None, None),
        P("curve", "group", None, None),
        P("curve", "group", None),
    )
    out_specs = P(None, "curve", "group", None)
    return jax.shard_map(local, mesh=mesh, in_specs=in_specs, out_specs=out_specs, check_vma=False)
```
